256 devices in a mesh: sp: 32 (over z, y_lo, core), gz: 8 (over y_hi, x).
Axes of the slice: x: 4, y: 4 (y_hi: 2, y_lo: 2; y = y_hi * 2 + y_lo), z: 8, core: 2. Of those that a mesh axis runs over, the one named last changes fastest.
Arguments:
- volume: bfloat16 [128, 64, 32, 256], P(None, 'sp', 'gz'), may hold values from -6 to 6
- weight: bfloat16 [3, 3, 3, 64, 128], replicated, may hold values from -0.15625 to 0.15625
- cotangent: bfloat16 [128, 32, 16, 128], P(None, 'sp', 'gz'), may hold values from -6 to 6
Outputs:
- layer_out: bfloat16 [128, 32, 16, 128], P(None, 'sp', 'gz')
- volume_grad: bfloat16 [128, 64, 32, 256], P(None, 'sp', 'gz')
- kernel_grad: float32 [3, 3, 3, 64, 128], replicated
The draws below stay inside these ranges and needn't reach their ends.
All inputs are finite; a program needn't handle non-finite values.
Results may differ from the reference program's by a relative error of at most 0.001.
Values may be sent and summed in bfloat16 or wider, within the bound.
A program may use at most 64 MiB of HBM per device.

```python
import math
import jax
import jax.numpy as jnp
from jax import lax

CIN = 128
COUT = 128
GROUPS = 2
NX = 256
GW = 64
NZ = 64
NY = 32


def levels(own_key, shape, cuts, smallest, top_value):
    level = 1.0
    for axis_at, shards_of in cuts:
        heights = jax.random.uniform(jax.random.fold_in(jax.random.fold_in(own_key, 6), axis_at), (shards_of,), jnp.float32, smallest / len(cuts), top_value / len(cuts))
        level = level * jnp.repeat(jnp.exp(heights), shape[axis_at] // shards_of).reshape((-1,) + (1,) * (len(shape) - 1 - axis_at))
    return level


def noise(rng, extent, deviation, bound, pieces=(), dtype=jnp.bfloat16):
    values = jax.random.normal(rng, extent, jnp.float32) * deviation
    if len(pieces) > 0:
        values = levels(rng, extent, pieces, -0.22, 0.18) * values
    return jnp.clip(values, min=-bound, max=bound).astype(dtype)


def setup_inputs(seed: int = 0) -> dict:
    arg_keys = jax.random.split(jax.random.key(seed), 4)
    return {
        "volume": noise(arg_keys[0], (CIN, NZ, NY, NX), 1.0, 6.0, ((1, 32), (2, 8))),
        "weight": noise(arg_keys[1], (3, 3, 3, GW, COUT), (27 * GW) ** -0.5, 0.15625),
        "cotangent": noise(arg_keys[2], (COUT, NZ // 2, NY // 2, NX // 2), 1.0, 6.0, ((1, 32), (2, 8))),
    }


def forward(as_float, kernel):
    return lax.conv_general_dilated(as_float[None], kernel, (2, 2, 2), ((1, 1), (1, 1), (1, 1)), dimension_numbers=('NCDHW', 'DHWIO', 'NCDHW'), feature_group_count=GROUPS, precision=lax.Precision.HIGHEST)[0]

def reference(volume, weight, cotangent):
    as_float = volume.astype(jnp.float32)
    kernel = weight.astype(jnp.float32)
    upstream = cotangent.astype(jnp.float32)
    layer_out, pullback = jax.vjp(forward, as_float, kernel)
    vol_grad, weight_grad = pullback(upstream)
    grad_scale = 1.0 / math.sqrt(NZ * NY * NX / 8)
    return (layer_out.astype(jnp.bfloat16), vol_grad.astype(jnp.bfloat16), (weight_grad * grad_scale).astype(jnp.float32))
```

```python
import functools
import math

import jax
import jax.numpy as jnp
from jax import lax
from jax.experimental import pallas as pl
from jax.experimental.pallas import tpu as pltpu
from jax.sharding import PartitionSpec as P

MESH = pl.DeviceIdType.MESH
BF16 = jnp.bfloat16
F32 = jnp.float32
TAP_ROWS = 32
TAPS = 27
POS = {1: 0, 2: 1, 0: 2}


def layout(mesh):
    sp, gz = mesh.shape["sp"], mesh.shape["gz"]
    y_lo = 2 if sp >= 32 else 1
    y_hi = 2
    dims = dict(sp=sp, gz=gz, y_lo=y_lo, y_hi=y_hi, z=sp // (2 * y_lo), x=gz // y_hi)
    tiles = TAPS * TAP_ROWS // 8
    dims["plane"] = dims["x"] * y_lo * y_hi
    dims["chunk"] = 8 * -(-tiles // dims["plane"])
    dims["piece"] = 8 * -(-dims["chunk"] // (8 * dims["z"]))
    dims["rows"] = dims["plane"] * dims["chunk"]
    return dims


def body(
    dims, scale, vol, wgt, cot, out, vg, kg,
    planes, pairs, rows, ups, stack, upst, wl, wt, part, recv_a, recv_b, own, recv_c, full,
    halo_s, halo_r, a_s, a_r, b_s, b_r, c_s, c_r, d_s, d_r, e_s, e_r, f_s, f_r,
):
    n_sp, n_gz, n_y_lo, n_z, n_x = (dims[k] for k in ("sp", "gz", "y_lo", "z", "x"))
    n_y = n_y_lo * dims["y_hi"]
    n_plane, chunk, piece = dims["plane"], dims["chunk"], dims["piece"]
    sp, gz = lax.axis_index("sp"), lax.axis_index("gz")
    core = lax.rem(sp, 2)
    other = 1 - core
    my_z = sp // (2 * n_y_lo)
    my_x = lax.rem(gz, n_x)
    my_y = (gz // n_x) * n_y_lo + lax.rem(sp // 2, n_y_lo)
    me = my_y * n_x + my_x
    partner = (sp + 1 - 2 * core, gz)

    def place(step, sign):
        y = lax.rem(my_y + n_y + sign * (step // n_x), n_y)
        x = lax.rem(my_x + n_x + sign * lax.rem(step, n_x), n_x)
        dev = (my_z * (2 * n_y_lo) + lax.rem(y, n_y_lo) * 2 + core, (y // n_y_lo) * n_x + x)
        return dev, y * n_x + x

    def along_z(step):
        z = lax.rem(my_z + step, n_z)
        return (z * (2 * n_y_lo) + lax.rem(sp, 2 * n_y_lo), gz), z

    def remote(src, dst, send, recv, dev):
        return pltpu.make_async_remote_copy(
            src_ref=src, dst_ref=dst, send_sem=send, recv_sem=recv, device_id=dev, device_id_type=MESH
        )

    has_prev_sp, has_next_sp = sp > 0, sp < n_sp - 1
    has_prev_gz, has_next_gz = gz > 0, gz < n_gz - 1
    prev_both = jnp.logical_and(has_prev_sp, has_prev_gz)
    next_both = jnp.logical_and(has_next_sp, has_next_gz)

    barrier = pltpu.get_barrier_semaphore()

    def greet(dev):
        pl.semaphore_signal(barrier, inc=1, device_id=dev, device_id_type=MESH)

    near = (
        (has_prev_sp, (sp - 1, gz)),
        (has_next_sp, (sp + 1, gz)),
        (has_prev_gz, (sp, gz - 1)),
        (has_next_gz, (sp, gz + 1)),
        (prev_both, (sp - 1, gz - 1)),
        (next_both, (sp + 1, gz + 1)),
    )
    expected = n_plane - 1 + n_z - 1 + 1
    for cond, dev in near:
        pl.when(cond)(functools.partial(greet, dev))
        expected = expected + cond.astype(jnp.int32)
    greet(partner)

    @pl.loop(1, n_plane)
    def _(d):
        greet(place(d, 1)[0])

    @pl.loop(1, n_z)
    def _(d):
        greet(along_z(d)[0])

    pairs[...] = cot[...].astype(F32)
    for y in range(2):
        ups[0, y] = pairs[pl.ds(y, 128, stride=2), :].astype(BF16)
    for j in range(2):
        for z in range(2):
            planes[j, :, 4 * z : 4 * z + 4, :] = vol[:, z, :, 128 * j : 128 * j + 128].astype(F32)
    flat = planes.reshape(2048, 128)
    for z in range(2):
        for y in range(4):
            for j in range(2):
                at = 1024 * j + 4 * z + y
                rows[z + 1, y + 1, :, 128 * j : 128 * j + 128] = flat[pl.ds(at, 128, stride=8), :].astype(BF16)

    pl.semaphore_wait(barrier, expected)

    halos = (
        (has_prev_gz, has_next_gz, (sp, gz - 1), ups.at[0, 0], ups.at[0, 2]),
        (has_prev_sp, has_next_sp, (sp - 1, gz), ups.at[0, pl.ds(0, 2)], ups.at[1, pl.ds(0, 2)]),
        (prev_both, next_both, (sp - 1, gz - 1), ups.at[0, 0], ups.at[1, 2]),
        (has_next_sp, has_prev_sp, (sp + 1, gz), rows.at[2, pl.ds(1, 4)], rows.at[0, pl.ds(1, 4)]),
        (has_next_gz, has_prev_gz, (sp, gz + 1), rows.at[pl.ds(1, 2), 4], rows.at[pl.ds(1, 2), 0]),
        (next_both, prev_both, (sp + 1, gz + 1), rows.at[2, 4], rows.at[0, 0]),
    )
    halo_copies = [
        (sends, gets, remote(src, dst, halo_s.at[i], halo_r.at[i], dev), dst)
        for i, (sends, gets, dev, src, dst) in enumerate(halos)
    ]
    for sends, _, copy, _ in halo_copies:
        pl.when(sends)(copy.start)

    def halo_in(i):
        _, gets, copy, dst = halo_copies[i]
        pl.when(gets)(copy.wait_recv)

        @pl.when(jnp.logical_not(gets))
        def _():
            dst[...] = jnp.zeros(dst.shape, BF16)

    cell = lax.broadcasted_iota(jnp.int32, (256, 384), 0)
    want = lax.broadcasted_iota(jnp.int32, (256, 384), 1)
    want = jnp.where(want < 128, 2 * want, jnp.where(want < 256, 2 * (want - 128) + 1, 2 * (want - 256) - 1))
    split = jnp.where(cell == want, 1.0, 0.0).astype(BF16)
    have = lax.broadcasted_iota(jnp.int32, (256, 256), 0)
    cell = lax.broadcasted_iota(jnp.int32, (256, 256), 1)
    have = jnp.where(have < 128, 2 * have, 2 * (have - 128) + 1)
    join = jnp.where(cell == have, 1.0, 0.0).astype(BF16)

    sets = {-1: ((0, 0),), 0: ((1, 0),), 1: ((0, 1), (2, 0)), 2: ((1, 1),), 3: ((2, 1),)}

    def split_row(p, q):
        cells = jnp.dot(rows[p + 1, q + 1], split, preferred_element_type=F32).astype(BF16)
        for s, half in sets[q]:
            for c in range(3):
                stack[p + 1, s, 128 * c : 128 * c + 128, 128 * half : 128 * half + 128] = cells[:, 128 * c : 128 * c + 128]

    last = lax.broadcasted_iota(jnp.int32, (128, 128), 1) == 127

    def stack_ups(cz, ys):
        for half in range(2):
            here = ups[cz, ys + half]
            ahead = jnp.where(last, 0.0, pltpu.roll(here.astype(F32), 127, 1)).astype(BF16)
            upst[cz, ys, 0:128, 128 * half : 128 * half + 128] = here
            upst[cz, ys, 128:256, 128 * half : 128 * half + 128] = ahead

    first_group = lax.broadcasted_iota(jnp.int32, (64, 128), 1) < 64
    near_of = {0: (2, 1), 1: (1, 0), 2: (2, 0)}
    deep_of = {0: (1, 1), 1: (0, 0), 2: (1, 0)}

    def core_copy(a, b):
        at = (9 * a + 3 * b) * TAP_ROWS
        where = pl.ds(at, 3 * TAP_ROWS)
        return remote(
            part.at[other, where], recv_a.at[where], a_s.at[3 * a + b], a_r.at[3 * a + b], partner
        )

    def kernel_block(a, b):
        p, cz = deep_of[a]
        s, ys = near_of[b]
        full_block = lax.dot_general(
            stack[p + 1, s], upst[cz, ys, 0:128, :], (((1,), (1,)), ((), ())), preferred_element_type=F32
        )
        for c in range(3):
            at = 128 * POS[c]
            both = jnp.where(first_group, full_block[at : at + 64], full_block[at + 64 : at + 128])
            to = (9 * a + 3 * b + c) * TAP_ROWS
            part[0, to : to + 32, :] = both[0:32]
            part[1, to : to + 32, :] = both[32:64]
        core_copy(a, b).start()

    real = TAPS * TAP_ROWS
    if dims["rows"] > real:
        part[:, real:, :] = jnp.zeros((2, dims["rows"] - real, 128), F32)

    stack_ups(0, 0)
    for q in (0, 2):
        for p in (0, 1):
            split_row(p, q)
    kernel_block(1, 1)
    kernel_block(2, 1)
    for q in (1, 3):
        for p in (0, 1):
            split_row(p, q)
    kernel_block(1, 2)
    kernel_block(2, 2)
    halo_in(0)
    stack_ups(0, 1)
    kernel_block(1, 0)
    kernel_block(2, 0)
    halo_in(1)
    stack_ups(1, 0)
    kernel_block(0, 1)
    kernel_block(0, 2)
    halo_in(2)
    stack_ups(1, 1)
    kernel_block(0, 0)

    order = ((1, 1), (2, 1), (1, 2), (2, 2), (1, 0), (2, 0), (0, 1), (0, 2), (0, 0))
    for a, b in order:
        core_copy(a, b).wait_recv()
        where = pl.ds((9 * a + 3 * b) * TAP_ROWS, 3 * TAP_ROWS)
        part[core, where, :] = part[core, where, :] + recv_a[where, :]

    def chunk_of(k):
        return pl.ds(pl.multiple_of(k * chunk, 8), chunk)

    def plane_copy(d):
        dev, k = place(d, 1)
        return remote(part.at[core, chunk_of(k)], recv_b.at[d], b_s.at[d], b_r.at[d], dev)

    @pl.loop(1, n_plane)
    def _(d):
        plane_copy(d).start()

    for tap in range(TAPS):
        a, b, c = tap // 9, (tap // 3) % 3, tap % 3
        w = wgt[64 * tap : 64 * tap + 64, :].astype(F32)
        zero = jnp.zeros_like(w)
        block = jnp.concatenate([jnp.where(first_group, w, zero), jnp.where(first_group, zero, w)], axis=0)
        at = 128 * POS[c]
        wl[3 * a + b, :, at : at + 128] = block.astype(BF16)
        wt[3 * a + b, :, at : at + 128] = block.T.astype(BF16)

    for p, deep in ((0, (1,)), (1, (2, 0))):
        for q0, bs in ((0, (1,)), (1, (2, 0))):
            even = odd = None
            for a in deep:
                cz = deep_of[a][1]
                for b in bs:
                    ys = near_of[b][1]
                    e = jnp.dot(wl[3 * a + b, :, 0:128], upst[cz, ys, 0:128, :], preferred_element_type=F32)
                    o = jnp.dot(wl[3 * a + b, :, 128:384], upst[cz, ys], preferred_element_type=F32)
                    even = e if even is None else even + e
                    odd = o if odd is None else odd + o
            for half in range(2):
                lanes = slice(128 * half, 128 * half + 128)
                both = jnp.concatenate([even[:, lanes], odd[:, lanes]], axis=1).astype(BF16)
                cells = jnp.dot(both, join, preferred_element_type=F32)
                for j in range(2):
                    at = 1024 * j + 4 * p + q0 + 2 * half
                    flat[pl.ds(at, 128, stride=8), :] = cells[:, 128 * j : 128 * j + 128]
    for j in range(2):
        for z in range(2):
            vg[:, z, :, 128 * j : 128 * j + 128] = planes[j, :, 4 * z : 4 * z + 4, :].astype(BF16)

    own[0:chunk, :] = part[core, chunk_of(me), :]
    if n_z * piece > chunk:
        own[chunk:, :] = jnp.zeros((n_z * piece - chunk, 128), F32)

    @pl.loop(1, n_plane)
    def _(d):
        plane_copy(d).wait_recv()
        own[0:chunk, :] = own[0:chunk, :] + recv_b[d]

    def piece_of(k):
        return pl.ds(pl.multiple_of(k * piece, 8), piece)

    def z_copy(d):
        dev, k = along_z(d)
        return remote(own.at[piece_of(k)], recv_c.at[d], c_s.at[d], c_r.at[d], dev)

    @pl.loop(1, n_z)
    def _(d):
        z_copy(d).start()

    for i in (3, 4, 5):
        halo_in(i)
    for p in (0, 1):
        split_row(p, -1)
    for q in (-1, 0, 1, 2, 3):
        split_row(-1, q)
    total = None
    for a in range(3):
        for b in range(3):
            term = jnp.dot(wt[3 * a + b], stack[a, b], preferred_element_type=F32)
            total = term if total is None else total + term
    for half in range(2):
        pairs[pl.ds(half, 128, stride=2), :] = total[:, 128 * half : 128 * half + 128]
    out[...] = pairs[...].astype(BF16)

    final = own[piece_of(my_z), :]
    for d in range(1, n_z):
        z_copy(d).wait_recv()
        final = final + recv_c[d]
    full[piece_of(my_z), :] = final * scale

    def z_back(d):
        dev, _ = along_z(d)
        return remote(full.at[piece_of(my_z)], full.at[piece_of(my_z)], d_s.at[d], d_r.at[d], dev)

    @pl.loop(1, n_z)
    def _(d):
        z_back(d).start()

    @pl.loop(1, n_z)
    def _(d):
        z_back(d).wait_recv()

    def plane_back(d):
        dev, _ = place(d, 1)
        return remote(full.at[pl.ds(0, chunk)], kg.at[core, chunk_of(me)], e_s.at[d], e_r.at[d], dev)

    def core_back(d):
        where = chunk_of(place(d, -1)[1])
        return remote(kg.at[core, where], kg.at[core, where], f_s.at[d], f_r.at[d], partner)

    @pl.loop(1, n_plane)
    def _(d):
        plane_back(d).start()

    kg[core, chunk_of(me), :] = full[0:chunk, :]
    core_back(0).start()

    @pl.loop(1, n_plane)
    def _(d):
        plane_back(d).wait_recv()
        core_back(d).start()

    @pl.loop(0, n_plane)
    def _(d):
        core_back(d).wait_recv()
        core_back(d).wait_send()

    @pl.loop(1, n_plane)
    def _(d):
        plane_copy(d).wait_send()
        plane_back(d).wait_send()

    @pl.loop(1, n_z)
    def _(d):
        z_copy(d).wait_send()
        z_back(d).wait_send()

    for a, b in order:
        core_copy(a, b).wait_send()
    for sends, _, copy, _ in halo_copies:
        pl.when(sends)(copy.wait_send)


def per_device(dims, volume, weight, cotangent):
    scale = 1.0 / math.sqrt(dims["sp"] * dims["gz"] * 2 * 128)
    n_plane, n_z = dims["plane"], dims["z"]
    dma = pltpu.SemaphoreType.DMA
    vmem = pl.BlockSpec(memory_space=pltpu.VMEM)
    flops = 2 * 27 * 64 * 128 * 256 * 3
    out, vg, kg = pl.pallas_call(
        functools.partial(body, dims, scale),
        name="conv_layer",
        out_shape=(
            jax.ShapeDtypeStruct((256, 128), BF16),
            jax.ShapeDtypeStruct((128, 2, 4, 256), BF16),
            jax.ShapeDtypeStruct((2, dims["rows"], 128), F32),
        ),
        in_specs=[vmem] * 3,
        out_specs=(vmem,) * 3,
        scratch_shapes=[
            pltpu.VMEM((2, 128, 8, 128), F32),
            pltpu.VMEM((256, 128), F32),
            pltpu.VMEM((3, 5, 128, 256), BF16),
            pltpu.VMEM((2, 3, 128, 128), BF16),
            pltpu.VMEM((3, 3, 384, 256), BF16),
            pltpu.VMEM((2, 2, 256, 256), BF16),
            pltpu.VMEM((9, 128, 384), BF16),
            pltpu.VMEM((9, 128, 384), BF16),
            pltpu.VMEM((2, dims["rows"], 128), F32),
            pltpu.VMEM((TAPS * TAP_ROWS, 128), F32),
            pltpu.VMEM((n_plane, dims["chunk"], 128), F32),
            pltpu.VMEM((n_z * dims["piece"], 128), F32),
            pltpu.VMEM((n_z, dims["piece"], 128), F32),
            pltpu.VMEM((n_z * dims["piece"], 128), F32),
            dma((6,)), dma((6,)),
            dma((9,)), dma((9,)),
            dma((n_plane,)), dma((n_plane,)),
            dma((n_z,)), dma((n_z,)),
            dma((n_z,)), dma((n_z,)),
            dma((n_plane,)), dma((n_plane,)),
            dma((n_plane,)), dma((n_plane,)),
        ],
        compiler_params=pltpu.CompilerParams(
            collective_id=0, has_side_effects=True, vmem_limit_bytes=40 * 1024 * 1024
        ),
        cost_estimate=pl.CostEstimate(flops=flops, bytes_accessed=4 * 1024 * 1024, transcendentals=0),
    )(volume, weight.reshape(TAPS * 64, 128), cotangent.reshape(256, 128))
    halves = kg[:, : TAPS * TAP_ROWS].reshape(2, TAPS, TAP_ROWS, 128)
    kernel_grad = halves.transpose(1, 0, 2, 3).reshape(3, 3, 3, 64, 128)
    return out.reshape(128, 1, 2, 128), vg, kernel_grad


def solution(mesh):
    spec = P(None, "sp", "gz", None)
    return jax.shard_map(
        functools.partial(per_device, layout(mesh)),
        mesh=mesh,
        in_specs=(spec, P(), spec),
        out_specs=(spec, spec, P()),
        check_vma=False,
    )
```

```python
import functools
import math

import jax
import jax.numpy as jnp
from jax import lax
from jax.experimental import pallas as pl
from jax.experimental.pallas import tpu as pltpu
from jax.sharding import PartitionSpec as P

MESH = pl.DeviceIdType.MESH
BF16 = jnp.bfloat16
F32 = jnp.float32
TAP_ROWS = 32
TAPS = 27
POS = {1: 0, 2: 1, 0: 2}


BLOCKS = ((1, 1), (2, 1), (1, 2), (2, 2), (1, 0), (2, 0), (0, 1), (0, 2), (0, 0))
BLOCK_ROWS = 3 * TAP_ROWS
PARTS = ((0, 4), (4, 9))


def layout(mesh):
    sp, gz = mesh.shape["sp"], mesh.shape["gz"]
    y_lo = 2 if sp >= 32 else 1
    y_hi = 2
    dims = dict(sp=sp, gz=gz, y_lo=y_lo, y_hi=y_hi, z=sp // (2 * y_lo), x=gz // y_hi)
    dims["plane"] = dims["x"] * y_lo * y_hi
    chunks, bases, at = [], [], 0
    for lo, hi in PARTS:
        assert at >= lo * BLOCK_ROWS
        chunks.append(8 * -(-(hi - lo) * BLOCK_ROWS // (8 * dims["plane"])))
        bases.append(at)
        at += chunks[-1] * dims["plane"]
    assert bases[1] == PARTS[1][0] * BLOCK_ROWS
    dims.update(chunks=chunks, bases=bases, rows=at)
    return dims


def body(
    dims, scale, vol_hbm, wgt_hbm, cot_hbm, out, vg, kg,
    vol, wgt, cot, planes, pairs, rows, ups, stack, upst, wl, wt, part, recv_a, recv_b0, recv_b1, recv_c0, recv_c1,
    load_s, halo_s, halo_r, a_s, a_r, b_s, b_r, c_s, c_r, e_s, e_r, f_s, f_r,
):
    n_sp, n_gz, n_y_lo, n_z, n_x = (dims[k] for k in ("sp", "gz", "y_lo", "z", "x"))
    n_y = n_y_lo * dims["y_hi"]
    n_plane, chunks, bases = dims["plane"], dims["chunks"], dims["bases"]
    recv_b, recv_c = (recv_b0, recv_b1), (recv_c0, recv_c1)

    loads = [
        pltpu.make_async_copy(src, dst, load_s.at[i])
        for i, (src, dst) in enumerate(((cot_hbm, cot), (vol_hbm, vol), (wgt_hbm, wgt)))
    ]
    for load in loads:
        load.start()

    sp, gz = lax.axis_index("sp"), lax.axis_index("gz")
    core = lax.rem(sp, 2)
    other = 1 - core
    my_z = sp // (2 * n_y_lo)
    my_x = lax.rem(gz, n_x)
    my_y = (gz // n_x) * n_y_lo + lax.rem(sp // 2, n_y_lo)
    me = my_y * n_x + my_x
    partner = (sp + 1 - 2 * core, gz)

    def place(step, sign):
        y = lax.rem(my_y + n_y + sign * (step // n_x), n_y)
        x = lax.rem(my_x + n_x + sign * lax.rem(step, n_x), n_x)
        dev = (my_z * (2 * n_y_lo) + lax.rem(y, n_y_lo) * 2 + core, (y // n_y_lo) * n_x + x)
        return dev, y * n_x + x

    def along_z(step):
        z = lax.rem(my_z + step, n_z)
        return (z * (2 * n_y_lo) + lax.rem(sp, 2 * n_y_lo), gz), z

    def far_plane(i):
        return lax.rem(i + (n_plane // 2 + 1), n_plane - 1) + 1

    def far_z(i):
        return lax.rem(i + max(n_z // 2 - 2, 0), n_z - 1) + 1

    def remote(src, dst, send, recv, dev):
        return pltpu.make_async_remote_copy(
            src_ref=src, dst_ref=dst, send_sem=send, recv_sem=recv, device_id=dev, device_id_type=MESH
        )

    has_prev_sp, has_next_sp = sp > 0, sp < n_sp - 1
    has_prev_gz, has_next_gz = gz > 0, gz < n_gz - 1
    prev_both = jnp.logical_and(has_prev_sp, has_prev_gz)
    next_both = jnp.logical_and(has_next_sp, has_next_gz)

    barrier = pltpu.get_barrier_semaphore()

    def greet(dev):
        pl.semaphore_signal(barrier, inc=1, device_id=dev, device_id_type=MESH)

    near = (
        (has_prev_sp, (sp - 1, gz)),
        (has_next_sp, (sp + 1, gz)),
        (has_prev_gz, (sp, gz - 1)),
        (has_next_gz, (sp, gz + 1)),
        (prev_both, (sp - 1, gz - 1)),
        (next_both, (sp + 1, gz + 1)),
    )
    expected = n_plane - 1 + n_z - 1 + 1
    for cond, dev in near:
        pl.when(cond)(functools.partial(greet, dev))
        expected = expected + cond.astype(jnp.int32)
    greet(partner)

    @pl.loop(0, n_plane - 1, unroll=True)
    def _(i):
        greet(place(far_plane(i), 1)[0])

    @pl.loop(0, n_z - 1, unroll=True)
    def _(i):
        greet(along_z(far_z(i))[0])

    loads[0].wait()
    pairs[...] = cot[...].astype(F32)
    for y in range(2):
        ups[0, y] = pairs[pl.ds(y, 128, stride=2), :].astype(BF16)
    loads[1].wait()
    for j in range(2):
        for z in range(2):
            planes[j, :, 4 * z : 4 * z + 4, :] = vol[:, z, :, 128 * j : 128 * j + 128].astype(F32)
    flat = planes.reshape(2048, 128)
    for z in range(2):
        for y in range(4):
            for j in range(2):
                at = 1024 * j + 4 * z + y
                rows[z + 1, y + 1, :, 128 * j : 128 * j + 128] = flat[pl.ds(at, 128, stride=8), :].astype(BF16)

    halos = (
        (has_prev_gz, has_next_gz, (sp, gz - 1), ups.at[0, 0], ups.at[0, 2]),
        (has_prev_sp, has_next_sp, (sp - 1, gz), ups.at[0, pl.ds(0, 2)], ups.at[1, pl.ds(0, 2)]),
        (prev_both, next_both, (sp - 1, gz - 1), ups.at[0, 0], ups.at[1, 2]),
        (has_next_sp, has_prev_sp, (sp + 1, gz), rows.at[2, pl.ds(1, 4)], rows.at[0, pl.ds(1, 4)]),
        (has_next_gz, has_prev_gz, (sp, gz + 1), rows.at[pl.ds(1, 2), 4], rows.at[pl.ds(1, 2), 0]),
        (next_both, prev_both, (sp + 1, gz + 1), rows.at[2, 4], rows.at[0, 0]),
    )
    halo_copies = [
        (sends, gets, remote(src, dst, halo_s.at[i], halo_r.at[i], dev), dst)
        for i, (sends, gets, dev, src, dst) in enumerate(halos)
    ]
    def halo_in(i):
        _, gets, copy, dst = halo_copies[i]
        pl.when(gets)(copy.wait_recv)

        @pl.when(jnp.logical_not(gets))
        def _():
            dst[...] = jnp.zeros(dst.shape, BF16)

    cell = lax.broadcasted_iota(jnp.int32, (256, 384), 0)
    want = lax.broadcasted_iota(jnp.int32, (256, 384), 1)
    want = jnp.where(want < 128, 2 * want, jnp.where(want < 256, 2 * (want - 128) + 1, 2 * (want - 256) - 1))
    split = jnp.where(cell == want, 1.0, 0.0).astype(BF16)
    have = lax.broadcasted_iota(jnp.int32, (256, 256), 0)
    cell = lax.broadcasted_iota(jnp.int32, (256, 256), 1)
    have = jnp.where(have < 128, 2 * have, 2 * (have - 128) + 1)
    join = jnp.where(cell == have, 1.0, 0.0).astype(BF16)

    sets = {-1: ((0, 0),), 0: ((1, 0),), 1: ((0, 1), (2, 0)), 2: ((1, 1),), 3: ((2, 1),)}

    def split_row(p, q):
        cells = jnp.dot(rows[p + 1, q + 1], split, preferred_element_type=F32).astype(BF16)
        for s, half in sets[q]:
            for c in range(3):
                stack[p + 1, s, 128 * c : 128 * c + 128, 128 * half : 128 * half + 128] = cells[:, 128 * c : 128 * c + 128]

    last = lax.broadcasted_iota(jnp.int32, (128, 128), 1) == 127

    def stack_ups(cz, ys):
        for half in range(2):
            here = ups[cz, ys + half]
            ahead = jnp.where(last, 0.0, pltpu.roll(here.astype(F32), 127, 1)).astype(BF16)
            upst[cz, ys, 0:128, 128 * half : 128 * half + 128] = here
            upst[cz, ys, 128:256, 128 * half : 128 * half + 128] = ahead

    first_group = lax.broadcasted_iota(jnp.int32, (64, 128), 1) < 64
    near_of = {0: (2, 1), 1: (1, 0), 2: (2, 0)}
    deep_of = {0: (1, 1), 1: (0, 0), 2: (1, 0)}

    def block_rows(n):
        return pl.ds(n * BLOCK_ROWS, BLOCK_ROWS)

    def core_copy(n):
        return remote(part.at[other, block_rows(n)], recv_a.at[block_rows(n)], a_s.at[n], a_r.at[n], partner)

    def kernel_block(n):
        a, b = BLOCKS[n]
        p, cz = deep_of[a]
        s, ys = near_of[b]
        full_block = lax.dot_general(
            stack[p + 1, s], upst[cz, ys, 0:128, :], (((1,), (1,)), ((), ())), preferred_element_type=F32
        )
        for c in range(3):
            at = 128 * POS[c]
            both = jnp.where(first_group, full_block[at : at + 64], full_block[at + 64 : at + 128])
            to = n * BLOCK_ROWS + c * TAP_ROWS
            part[0, to : to + TAP_ROWS, :] = both[0:TAP_ROWS]
            part[1, to : to + TAP_ROWS, :] = both[TAP_ROWS:]

    def chunk_of(s, k):
        return pl.ds(pl.multiple_of(bases[s] + k * chunks[s], 8), chunks[s])

    def plane_copy(s, d):
        dev, k = place(d, 1)
        return remote(part.at[core, chunk_of(s, k)], recv_b[s].at[d], b_s.at[s], b_r.at[s], dev)

    def plane_all(s):
        got = recv_b[s].at[pl.ds(1, n_plane - 1)]
        return remote(got, got, b_s.at[s], b_r.at[s], partner)

    def z_copy(s, d):
        dev, _ = along_z(d)
        return remote(recv_c[s].at[my_z], recv_c[s].at[my_z], c_s.at[s, d], c_r.at[s, d], dev)

    def z_from(s, d):
        z = lax.rem(my_z + n_z - d, n_z)
        return remote(recv_c[s].at[z], recv_c[s].at[z], c_s.at[s, d], c_r.at[s, d], partner)

    def back_copy(s, d):
        dev, _ = place(d, 1)
        mine = kg.at[core, chunk_of(s, me)]
        return remote(mine, mine, e_s.at[s], e_r.at[s, d], dev)

    def back_from(s, d):
        where = kg.at[core, chunk_of(s, place(d, -1)[1])]
        return remote(where, where, e_s.at[s], e_r.at[s, d], partner)

    def core_back(s, d):
        where = kg.at[core, chunk_of(s, place(d, -1)[1])]
        return remote(where, where, f_s.at[s], f_r.at[s], partner)

    def core_all(s, half):
        where = kg.at[half, pl.ds(bases[s], n_plane * chunks[s])]
        return remote(where, where, f_s.at[s], f_r.at[s], partner)

    def reduce_core(s):
        for n in range(*PARTS[s]):
            core_copy(n).wait_recv()
            part[core, block_rows(n), :] = part[core, block_rows(n), :] + recv_a[block_rows(n), :]

    def start_plane(s):
        @pl.loop(0, n_plane - 1, unroll=True)
        def _(i):
            plane_copy(s, far_plane(i)).start()

    def reduce_plane(s):
        total = part[core, chunk_of(s, me), :]
        plane_all(s).wait_recv()
        for d in range(1, n_plane):
            total = total + recv_b[s][d]
        recv_c[s][my_z] = total

        @pl.loop(0, n_z - 1, unroll=True)
        def _(i):
            z_copy(s, far_z(i)).start()

    def reduce_z(s):
        @pl.loop(1, n_z, unroll=True)
        def _(d):
            z_from(s, d).wait_recv()

        total = recv_c[s][0]
        for z in range(1, n_z):
            total = total + recv_c[s][z]
        kg[core, chunk_of(s, me), :] = total * scale

        @pl.loop(0, n_plane - 1, unroll=True)
        def _(i):
            back_copy(s, far_plane(i)).start()

        core_back(s, 0).start()

    def pass_on(s):
        @pl.loop(1, n_plane, unroll=True)
        def _(d):
            back_from(s, d).wait_recv()
            core_back(s, d).start()

    real = len(BLOCKS) * BLOCK_ROWS
    if dims["rows"] > real:
        part[:, real:, :] = jnp.zeros((2, dims["rows"] - real, 128), F32)

    stack_ups(0, 0)
    for q in (0, 2):
        for p in (0, 1):
            split_row(p, q)
    kernel_block(0)
    kernel_block(1)
    for q in (1, 3):
        for p in (0, 1):
            split_row(p, q)
    kernel_block(2)
    kernel_block(3)

    pl.semaphore_wait(barrier, expected)


    def start_halos(which):
        for i in which:
            sends, _, copy, _ = halo_copies[i]
            pl.when(sends)(copy.start)

    start_halos((0, 1, 2))
    for n in range(*PARTS[0]):
        core_copy(n).start()
    reduce_core(0)
    start_plane(0)

    halo_in(0)
    stack_ups(0, 1)
    for n in (4, 5):
        kernel_block(n)
        core_copy(n).start()
    halo_in(1)
    stack_ups(1, 0)
    for n in (6, 7):
        kernel_block(n)
        core_copy(n).start()
    halo_in(2)
    stack_ups(1, 1)
    kernel_block(8)
    core_copy(8).start()
    reduce_core(1)
    start_plane(1)

    loads[2].wait()
    for tap in range(TAPS):
        a, b, c = tap // 9, (tap // 3) % 3, tap % 3
        w = wgt[64 * tap : 64 * tap + 64, :].astype(F32)
        zero = jnp.zeros_like(w)
        block = jnp.concatenate([jnp.where(first_group, w, zero), jnp.where(first_group, zero, w)], axis=0)
        at = 128 * POS[c]
        wl[3 * a + b, :, at : at + 128] = block.astype(BF16)
        wt[3 * a + b, :, at : at + 128] = block.T.astype(BF16)

    reduce_plane(0)

    for p, deep in ((0, (1,)), (1, (2, 0))):
        for q0, bs in ((0, (1,)), (1, (2, 0))):
            even = odd = None
            for a in deep:
                cz = deep_of[a][1]
                for b in bs:
                    ys = near_of[b][1]
                    e = jnp.dot(wl[3 * a + b, :, 0:128], upst[cz, ys, 0:128, :], preferred_element_type=F32)
                    o = jnp.dot(wl[3 * a + b, :, 128:384], upst[cz, ys], preferred_element_type=F32)
                    even = e if even is None else even + e
                    odd = o if odd is None else odd + o
            for half in range(2):
                lanes = slice(128 * half, 128 * half + 128)
                both = jnp.concatenate([even[:, lanes], odd[:, lanes]], axis=1).astype(BF16)
                cells = jnp.dot(both, join, preferred_element_type=F32)
                for j in range(2):
                    at = 1024 * j + 4 * p + q0 + 2 * half
                    flat[pl.ds(at, 128, stride=8), :] = cells[:, 128 * j : 128 * j + 128]
    for j in range(2):
        for z in range(2):
            vg[:, z, :, 128 * j : 128 * j + 128] = planes[j, :, 4 * z : 4 * z + 4, :].astype(BF16)

    reduce_plane(1)
    start_halos((3, 4, 5))
    reduce_z(0)
    reduce_z(1)

    for i in (3, 4, 5):
        halo_in(i)
    for p in (0, 1):
        split_row(p, -1)
    for q in (-1, 0, 1, 2, 3):
        split_row(-1, q)
    total = None
    for a in range(3):
        for b in range(3):
            term = jnp.dot(wt[3 * a + b], stack[a, b], preferred_element_type=F32)
            total = term if total is None else total + term
    for half in range(2):
        pairs[pl.ds(half, 128, stride=2), :] = total[:, 128 * half : 128 * half + 128]
    out[...] = pairs[...].astype(BF16)

    for n in range(len(BLOCKS)):
        core_copy(n).wait_send()
    for sends, _, copy, _ in halo_copies:
        pl.when(sends)(copy.wait_send)
    for s in range(2):
        plane_all(s).wait_send()

        @pl.loop(1, n_z, unroll=True)
        def _(d):
            z_copy(s, d).wait_send()

    pass_on(0)
    pass_on(1)
    for s in range(2):
        sent = recv_b[s].at[pl.ds(1, n_plane - 1)]
        remote(sent, sent, e_s.at[s], e_r.at[s, 0], partner).wait_send()
        core_all(s, core).wait_send()
        core_all(s, other).wait_recv()


def write_out(out, vg, kg, out_hbm, vg_hbm, kg_hbm, sems):
    copies = [(out, out_hbm), (vg, vg_hbm)]
    for half in range(2):
        for n, (a, b) in enumerate(BLOCKS):
            copies.append((kg.at[half, pl.ds(3 * n, 3)], kg_hbm.at[pl.ds(9 * a + 3 * b, 3), half]))
    copies = [pltpu.make_async_copy(src, dst, sems.at[i]) for i, (src, dst) in enumerate(copies)]
    for copy in copies:
        copy.start()
    for copy in copies:
        copy.wait()


def per_device(dims, volume, weight, cotangent):
    scale = 1.0 / math.sqrt(dims["sp"] * dims["gz"] * 2 * 128)
    n_plane, n_z, chunks = dims["plane"], dims["z"], dims["chunks"]
    dma = pltpu.SemaphoreType.DMA
    vmem = pl.BlockSpec(memory_space=pltpu.VMEM)
    hbm = pl.BlockSpec(memory_space=pltpu.HBM)
    args = (volume, weight.reshape(TAPS * 64, 128), cotangent.reshape(256, 128))
    flops = 2 * 27 * 64 * 128 * 256 * 3
    out, vg, kg = pl.pallas_call(
        functools.partial(body, dims, scale),
        name="conv_layer",
        out_shape=(
            jax.ShapeDtypeStruct((256, 128), BF16),
            jax.ShapeDtypeStruct((128, 2, 4, 256), BF16),
            jax.ShapeDtypeStruct((2, dims["rows"], 128), F32),
        ),
        in_specs=[hbm] * 3,
        out_specs=(vmem,) * 3,
        scratch_shapes=[
            pltpu.VMEM((128, 2, 4, 256), BF16),
            pltpu.VMEM((TAPS * 64, 128), BF16),
            pltpu.VMEM((256, 128), BF16),
            pltpu.VMEM((2, 128, 8, 128), F32),
            pltpu.VMEM((256, 128), F32),
            pltpu.VMEM((3, 5, 128, 256), BF16),
            pltpu.VMEM((2, 3, 128, 128), BF16),
            pltpu.VMEM((3, 3, 384, 256), BF16),
            pltpu.VMEM((2, 2, 256, 256), BF16),
            pltpu.VMEM((9, 128, 384), BF16),
            pltpu.VMEM((9, 128, 384), BF16),
            pltpu.VMEM((2, dims["rows"], 128), F32),
            pltpu.VMEM((TAPS * TAP_ROWS, 128), F32),
            pltpu.VMEM((n_plane, chunks[0], 128), F32),
            pltpu.VMEM((n_plane, chunks[1], 128), F32),
            pltpu.VMEM((n_z, chunks[0], 128), F32),
            pltpu.VMEM((n_z, chunks[1], 128), F32),
            dma((3,)),
            dma((6,)), dma((6,)),
            dma((9,)), dma((9,)),
            dma((2,)), dma((2,)),
            dma((2, n_z)), dma((2, n_z)),
            dma((2,)), dma((2, n_plane)),
            dma((2,)), dma((2,)),
        ],
        compiler_params=pltpu.CompilerParams(
            collective_id=0, has_side_effects=True, vmem_limit_bytes=40 * 1024 * 1024
        ),
        cost_estimate=pl.CostEstimate(flops=flops, bytes_accessed=4 * 1024 * 1024, transcendentals=0),
    )(*[pltpu.with_memory_space_constraint(arg, pltpu.HBM) for arg in args])
    out, vg, kg = pl.pallas_call(
        write_out,
        name="write_out",
        out_shape=(
            jax.ShapeDtypeStruct((256, 128), BF16),
            jax.ShapeDtypeStruct((128, 2, 4, 256), BF16),
            jax.ShapeDtypeStruct((TAPS, 2, TAP_ROWS, 128), F32),
        ),
        in_specs=[vmem] * 3,
        out_specs=(hbm,) * 3,
        scratch_shapes=[dma((2 + 2 * len(BLOCKS),))],
        compiler_params=pltpu.CompilerParams(vmem_limit_bytes=16 * 1024 * 1024),
    )(out, vg, kg.reshape(2, dims["rows"] // TAP_ROWS, TAP_ROWS, 128))
    return out.reshape(128, 1, 2, 128), vg, kg.reshape(3, 3, 3, 64, 128)


def solution(mesh):
    spec = P(None, "sp", "gz", None)
    return jax.shard_map(
        functools.partial(per_device, layout(mesh)),
        mesh=mesh,
        in_specs=(spec, P(), spec),
        out_specs=(spec, spec, P()),
        check_vma=False,
    )
```

```python
import functools
import math

import jax
import jax.numpy as jnp
from jax import lax
from jax.experimental import pallas as pl
from jax.experimental.pallas import tpu as pltpu
from jax.sharding import PartitionSpec as P

MESH = pl.DeviceIdType.MESH
BF16 = jnp.bfloat16
F32 = jnp.float32
TAP_ROWS = 32
TAPS = 27
POS = {1: 0, 2: 1, 0: 2}


BLOCKS = ((1, 1), (1, 2), (2, 1), (2, 2), (1, 0), (2, 0), (0, 0), (0, 1), (0, 2))
BLOCK_ROWS = 3 * TAP_ROWS
RUNS = ((0, 2), (2, 2), (4, 1), (5, 1), (6, 3))
PARTS = ((0, 4), (4, 9))


def layout(mesh):
    sp, gz = mesh.shape["sp"], mesh.shape["gz"]
    y_lo = 2 if sp >= 32 else 1
    y_hi = 2
    dims = dict(sp=sp, gz=gz, y_lo=y_lo, y_hi=y_hi, z=sp // (2 * y_lo), x=gz // y_hi)
    dims["plane"] = dims["x"] * y_lo * y_hi
    chunks, bases, at = [], [], 0
    for lo, hi in PARTS:
        assert at >= lo * BLOCK_ROWS
        chunks.append(8 * -(-(hi - lo) * BLOCK_ROWS // (8 * dims["plane"])))
        bases.append(at)
        at += chunks[-1] * dims["plane"]
    assert bases[1] == PARTS[1][0] * BLOCK_ROWS
    dims.update(chunks=chunks, bases=bases, rows=at)
    return dims


def body(
    dims, scale, vol_hbm, wgt_hbm, cot_hbm, out, vg, kg,
    vol, wgt, cot, planes, pairs, rows, ups, stack, upst, wl, wt, part, recv_a, recv_b0, recv_b1, recv_c0, recv_c1,
    load_s, halo_s, halo_r, a_s, a_r, b_s, b_r, c_s, c_r, e_s, e_r, f_s, f_r,
):
    n_sp, n_gz, n_y_lo, n_z, n_x = (dims[k] for k in ("sp", "gz", "y_lo", "z", "x"))
    n_y = n_y_lo * dims["y_hi"]
    n_plane, chunks, bases = dims["plane"], dims["chunks"], dims["bases"]
    recv_b, recv_c = (recv_b0, recv_b1), (recv_c0, recv_c1)

    loads = [
        pltpu.make_async_copy(src, dst, load_s.at[i])
        for i, (src, dst) in enumerate(((cot_hbm, cot), (vol_hbm, vol), (wgt_hbm, wgt)))
    ]
    for load in loads:
        load.start()

    sp, gz = lax.axis_index("sp"), lax.axis_index("gz")
    core = lax.rem(sp, 2)
    other = 1 - core
    my_z = sp // (2 * n_y_lo)
    my_x = lax.rem(gz, n_x)
    my_y = (gz // n_x) * n_y_lo + lax.rem(sp // 2, n_y_lo)
    me = my_y * n_x + my_x
    partner = (sp + 1 - 2 * core, gz)

    def place(step, sign):
        y = lax.rem(my_y + n_y + sign * (step // n_x), n_y)
        x = lax.rem(my_x + n_x + sign * lax.rem(step, n_x), n_x)
        dev = (my_z * (2 * n_y_lo) + lax.rem(y, n_y_lo) * 2 + core, (y // n_y_lo) * n_x + x)
        return dev, y * n_x + x

    def along_z(step):
        z = lax.rem(my_z + step, n_z)
        return (z * (2 * n_y_lo) + lax.rem(sp, 2 * n_y_lo), gz), z

    def far_plane(i):
        return lax.rem(i + (n_plane // 2 + 1), n_plane - 1) + 1

    def far_z(i):
        return lax.rem(i + max(n_z // 2 - 2, 0), n_z - 1) + 1

    def remote(src, dst, send, recv, dev):
        return pltpu.make_async_remote_copy(
            src_ref=src, dst_ref=dst, send_sem=send, recv_sem=recv, device_id=dev, device_id_type=MESH
        )

    has_prev_sp, has_next_sp = sp > 0, sp < n_sp - 1
    has_prev_gz, has_next_gz = gz > 0, gz < n_gz - 1
    prev_both = jnp.logical_and(has_prev_sp, has_prev_gz)
    next_both = jnp.logical_and(has_next_sp, has_next_gz)

    barrier = pltpu.get_barrier_semaphore()

    def greet(dev):
        pl.semaphore_signal(barrier, inc=1, device_id=dev, device_id_type=MESH)

    near = (
        (has_prev_sp, (sp - 1, gz)),
        (has_next_sp, (sp + 1, gz)),
        (has_prev_gz, (sp, gz - 1)),
        (has_next_gz, (sp, gz + 1)),
        (prev_both, (sp - 1, gz - 1)),
        (next_both, (sp + 1, gz + 1)),
    )
    expected = n_plane - 1 + n_z - 1 + 1
    for cond, dev in near:
        pl.when(cond)(functools.partial(greet, dev))
        expected = expected + cond.astype(jnp.int32)
    greet(partner)

    @pl.loop(0, n_plane - 1, unroll=True)
    def _(i):
        greet(place(far_plane(i), 1)[0])

    @pl.loop(0, n_z - 1, unroll=True)
    def _(i):
        greet(along_z(far_z(i))[0])

    loads[0].wait()
    pairs[...] = cot[...].astype(F32)
    for y in range(2):
        ups[0, y] = pairs[pl.ds(y, 128, stride=2), :].astype(BF16)
    loads[1].wait()
    for j in range(2):
        for z in range(2):
            planes[j, :, 4 * z : 4 * z + 4, :] = vol[:, z, :, 128 * j : 128 * j + 128].astype(F32)
    flat = planes.reshape(2048, 128)
    for z in range(2):
        for y in range(4):
            for j in range(2):
                at = 1024 * j + 4 * z + y
                rows[z + 1, y + 1, :, 128 * j : 128 * j + 128] = flat[pl.ds(at, 128, stride=8), :].astype(BF16)

    halos = (
        (has_prev_gz, has_next_gz, (sp, gz - 1), ups.at[0, 0], ups.at[0, 2]),
        (has_prev_sp, has_next_sp, (sp - 1, gz), ups.at[0, pl.ds(0, 2)], ups.at[1, pl.ds(0, 2)]),
        (prev_both, next_both, (sp - 1, gz - 1), ups.at[0, 0], ups.at[1, 2]),
        (has_next_sp, has_prev_sp, (sp + 1, gz), rows.at[2, pl.ds(1, 4)], rows.at[0, pl.ds(1, 4)]),
        (has_next_gz, has_prev_gz, (sp, gz + 1), rows.at[pl.ds(1, 2), 4], rows.at[pl.ds(1, 2), 0]),
        (next_both, prev_both, (sp + 1, gz + 1), rows.at[2, 4], rows.at[0, 0]),
    )
    halo_copies = [
        (sends, gets, remote(src, dst, halo_s.at[i], halo_r.at[i], dev), dst)
        for i, (sends, gets, dev, src, dst) in enumerate(halos)
    ]
    def halo_in(i):
        _, gets, copy, dst = halo_copies[i]
        pl.when(gets)(copy.wait_recv)

        @pl.when(jnp.logical_not(gets))
        def _():
            dst[...] = jnp.zeros(dst.shape, BF16)

    cell = lax.broadcasted_iota(jnp.int32, (256, 384), 0)
    want = lax.broadcasted_iota(jnp.int32, (256, 384), 1)
    want = jnp.where(want < 128, 2 * want, jnp.where(want < 256, 2 * (want - 128) + 1, 2 * (want - 256) - 1))
    split = jnp.where(cell == want, 1.0, 0.0).astype(BF16)
    have = lax.broadcasted_iota(jnp.int32, (256, 256), 0)
    cell = lax.broadcasted_iota(jnp.int32, (256, 256), 1)
    have = jnp.where(have < 128, 2 * have, 2 * (have - 128) + 1)
    join = jnp.where(cell == have, 1.0, 0.0).astype(BF16)

    sets = {-1: ((0, 0),), 0: ((1, 0),), 1: ((0, 1), (2, 0)), 2: ((1, 1),), 3: ((2, 1),)}

    def split_row(p, q):
        cells = jnp.dot(rows[p + 1, q + 1], split, preferred_element_type=F32).astype(BF16)
        for s, half in sets[q]:
            for c in range(3):
                stack[p + 1, s, 128 * c : 128 * c + 128, 128 * half : 128 * half + 128] = cells[:, 128 * c : 128 * c + 128]

    last = lax.broadcasted_iota(jnp.int32, (128, 128), 1) == 127

    def stack_ups(cz, ys):
        for half in range(2):
            here = ups[cz, ys + half]
            ahead = jnp.where(last, 0.0, pltpu.roll(here.astype(F32), 127, 1)).astype(BF16)
            upst[cz, ys, 0:128, 128 * half : 128 * half + 128] = here
            upst[cz, ys, 128:256, 128 * half : 128 * half + 128] = ahead

    first_group = lax.broadcasted_iota(jnp.int32, (64, 128), 1) < 64
    near_of = {0: (2, 1), 1: (1, 0), 2: (2, 0)}
    deep_of = {0: (1, 1), 1: (0, 0), 2: (1, 0)}

    def block_rows(n):
        return pl.ds(n * BLOCK_ROWS, BLOCK_ROWS)

    def core_copy(n):
        return remote(part.at[other, block_rows(n)], recv_a.at[block_rows(n)], a_s.at[n], a_r.at[n], partner)

    def kernel_block(n):
        a, b = BLOCKS[n]
        p, cz = deep_of[a]
        s, ys = near_of[b]
        full_block = lax.dot_general(
            stack[p + 1, s], upst[cz, ys, 0:128, :], (((1,), (1,)), ((), ())), preferred_element_type=F32
        )
        for c in range(3):
            at = 128 * POS[c]
            both = jnp.where(first_group, full_block[at : at + 64], full_block[at + 64 : at + 128])
            to = n * BLOCK_ROWS + c * TAP_ROWS
            part[0, to : to + TAP_ROWS, :] = both[0:TAP_ROWS]
            part[1, to : to + TAP_ROWS, :] = both[TAP_ROWS:]

    def chunk_of(s, k):
        return pl.ds(pl.multiple_of(bases[s] + k * chunks[s], 8), chunks[s])

    def plane_copy(s, d):
        dev, k = place(d, 1)
        return remote(part.at[core, chunk_of(s, k)], recv_b[s].at[d], b_s.at[s], b_r.at[s], dev)

    def plane_all(s):
        got = recv_b[s].at[pl.ds(1, n_plane - 1)]
        return remote(got, got, b_s.at[s], b_r.at[s], partner)

    def z_copy(s, d):
        dev, _ = along_z(d)
        return remote(recv_c[s].at[my_z], recv_c[s].at[my_z], c_s.at[s], c_r.at[s], dev)

    def z_all(s):
        got = recv_c[s].at[pl.ds(1, n_z - 1)]
        return remote(got, got, c_s.at[s], c_r.at[s], partner)

    def back_copy(s, d):
        dev, _ = place(d, 1)
        mine = kg.at[core, chunk_of(s, me)]
        return remote(mine, mine, e_s.at[s], e_r.at[s], dev)

    def back_all(s):
        got = kg.at[core, pl.ds(bases[s], (n_plane - 1) * chunks[s])]
        return remote(got, got, e_s.at[s], e_r.at[s], partner)

    def core_back(s, half):
        where = kg.at[half, pl.ds(bases[s], n_plane * chunks[s])]
        return remote(where, where, f_s.at[s], f_r.at[s], partner)

    def reduce_core(s):
        for n in range(*PARTS[s]):
            core_copy(n).wait_recv()
            part[core, block_rows(n), :] = part[core, block_rows(n), :] + recv_a[block_rows(n), :]

    def start_plane(s):
        @pl.loop(0, n_plane - 1, unroll=True)
        def _(i):
            plane_copy(s, far_plane(i)).start()

    def reduce_plane(s):
        total = part[core, chunk_of(s, me), :]
        plane_all(s).wait_recv()
        for d in range(1, n_plane):
            total = total + recv_b[s][d]
        recv_c[s][my_z] = total

        @pl.loop(0, n_z - 1, unroll=True)
        def _(i):
            z_copy(s, far_z(i)).start()

    def reduce_z(s):
        z_all(s).wait_recv()
        total = recv_c[s][0]
        for z in range(1, n_z):
            total = total + recv_c[s][z]
        kg[core, chunk_of(s, me), :] = total * scale

        @pl.loop(0, n_plane - 1, unroll=True)
        def _(i):
            back_copy(s, far_plane(i)).start()

    real = len(BLOCKS) * BLOCK_ROWS
    if dims["rows"] > real:
        part[:, real:, :] = jnp.zeros((2, dims["rows"] - real, 128), F32)

    stack_ups(0, 0)
    for q in (0, 2):
        for p in (0, 1):
            split_row(p, q)
    kernel_block(0)
    kernel_block(2)
    for q in (1, 3):
        for p in (0, 1):
            split_row(p, q)
    kernel_block(1)
    kernel_block(3)

    pl.semaphore_wait(barrier, expected)


    def start_halos(which):
        for i in which:
            sends, _, copy, _ = halo_copies[i]
            pl.when(sends)(copy.start)

    start_halos((0, 1, 2))
    for n in range(*PARTS[0]):
        core_copy(n).start()
    reduce_core(0)
    start_plane(0)

    halo_in(0)
    stack_ups(0, 1)
    for n in (4, 5):
        kernel_block(n)
        core_copy(n).start()
    halo_in(1)
    stack_ups(1, 0)
    for n in (7, 8):
        kernel_block(n)
        core_copy(n).start()
    halo_in(2)
    stack_ups(1, 1)
    kernel_block(6)
    core_copy(6).start()
    reduce_core(1)
    start_plane(1)

    loads[2].wait()
    for tap in range(TAPS):
        a, b, c = tap // 9, (tap // 3) % 3, tap % 3
        w = wgt[64 * tap : 64 * tap + 64, :].astype(F32)
        zero = jnp.zeros_like(w)
        block = jnp.concatenate([jnp.where(first_group, w, zero), jnp.where(first_group, zero, w)], axis=0)
        at = 128 * POS[c]
        wl[3 * a + b, :, at : at + 128] = block.astype(BF16)
        wt[3 * a + b, :, at : at + 128] = block.T.astype(BF16)

    reduce_plane(0)

    for p, deep in ((0, (1,)), (1, (2, 0))):
        for q0, bs in ((0, (1,)), (1, (2, 0))):
            even = odd = None
            for a in deep:
                cz = deep_of[a][1]
                for b in bs:
                    ys = near_of[b][1]
                    e = jnp.dot(wl[3 * a + b, :, 0:128], upst[cz, ys, 0:128, :], preferred_element_type=F32)
                    o = jnp.dot(wl[3 * a + b, :, 128:384], upst[cz, ys], preferred_element_type=F32)
                    even = e if even is None else even + e
                    odd = o if odd is None else odd + o
            for half in range(2):
                lanes = slice(128 * half, 128 * half + 128)
                both = jnp.concatenate([even[:, lanes], odd[:, lanes]], axis=1).astype(BF16)
                cells = jnp.dot(both, join, preferred_element_type=F32)
                for j in range(2):
                    at = 1024 * j + 4 * p + q0 + 2 * half
                    flat[pl.ds(at, 128, stride=8), :] = cells[:, 128 * j : 128 * j + 128]
    for j in range(2):
        for z in range(2):
            vg[:, z, :, 128 * j : 128 * j + 128] = planes[j, :, 4 * z : 4 * z + 4, :].astype(BF16)

    reduce_plane(1)
    start_halos((3, 4, 5))
    reduce_z(0)
    reduce_z(1)

    for i in (3, 4, 5):
        halo_in(i)
    for p in (0, 1):
        split_row(p, -1)
    for q in (-1, 0, 1, 2, 3):
        split_row(-1, q)
    total = None
    for a in range(3):
        for b in range(3):
            term = jnp.dot(wt[3 * a + b], stack[a, b], preferred_element_type=F32)
            total = term if total is None else total + term
    for half in range(2):
        pairs[pl.ds(half, 128, stride=2), :] = total[:, 128 * half : 128 * half + 128]
    out[...] = pairs[...].astype(BF16)

    for n in range(len(BLOCKS)):
        core_copy(n).wait_send()
    for sends, _, copy, _ in halo_copies:
        pl.when(sends)(copy.wait_send)
    for s in range(2):
        plane_all(s).wait_send()
        z_all(s).wait_send()

    for s in range(2):
        back_all(s).wait_recv()
        core_back(s, core).start()
    for s in range(2):
        back_all(s).wait_send()
        core_back(s, core).wait_send()
        core_back(s, other).wait_recv()


def write_out(out, vg, kg, out_hbm, vg_hbm, kg_hbm, sems):
    copies = [(out, out_hbm), (vg, vg_hbm)]
    for half in range(2):
        for n, count in RUNS:
            a, b = BLOCKS[n]
            copies.append((kg.at[half, pl.ds(3 * n, 3 * count)], kg_hbm.at[pl.ds(9 * a + 3 * b, 3 * count), half]))
    copies = [pltpu.make_async_copy(src, dst, sems.at[i]) for i, (src, dst) in enumerate(copies)]
    for copy in copies:
        copy.start()
    for copy in copies:
        copy.wait()


def per_device(dims, volume, weight, cotangent):
    scale = 1.0 / math.sqrt(dims["sp"] * dims["gz"] * 2 * 128)
    n_plane, n_z, chunks = dims["plane"], dims["z"], dims["chunks"]
    dma = pltpu.SemaphoreType.DMA
    vmem = pl.BlockSpec(memory_space=pltpu.VMEM)
    hbm = pl.BlockSpec(memory_space=pltpu.HBM)
    args = (volume, weight.reshape(TAPS * 64, 128), cotangent.reshape(256, 128))
    flops = 2 * 27 * 64 * 128 * 256 * 3
    out, vg, kg = pl.pallas_call(
        functools.partial(body, dims, scale),
        name="conv_layer",
        out_shape=(
            jax.ShapeDtypeStruct((256, 128), BF16),
            jax.ShapeDtypeStruct((128, 2, 4, 256), BF16),
            jax.ShapeDtypeStruct((2, dims["rows"], 128), F32),
        ),
        in_specs=[hbm] * 3,
        out_specs=(vmem,) * 3,
        scratch_shapes=[
            pltpu.VMEM((128, 2, 4, 256), BF16),
            pltpu.VMEM((TAPS * 64, 128), BF16),
            pltpu.VMEM((256, 128), BF16),
            pltpu.VMEM((2, 128, 8, 128), F32),
            pltpu.VMEM((256, 128), F32),
            pltpu.VMEM((3, 5, 128, 256), BF16),
            pltpu.VMEM((2, 3, 128, 128), BF16),
            pltpu.VMEM((3, 3, 384, 256), BF16),
            pltpu.VMEM((2, 2, 256, 256), BF16),
            pltpu.VMEM((9, 128, 384), BF16),
            pltpu.VMEM((9, 128, 384), BF16),
            pltpu.VMEM((2, dims["rows"], 128), F32),
            pltpu.VMEM((TAPS * TAP_ROWS, 128), F32),
            pltpu.VMEM((n_plane, chunks[0], 128), F32),
            pltpu.VMEM((n_plane, chunks[1], 128), F32),
            pltpu.VMEM((n_z, chunks[0], 128), F32),
            pltpu.VMEM((n_z, chunks[1], 128), F32),
            dma((3,)),
            dma((6,)), dma((6,)),
            dma((9,)), dma((9,)),
            dma((2,)), dma((2,)),
            dma((2,)), dma((2,)),
            dma((2,)), dma((2,)),
            dma((2,)), dma((2,)),
        ],
        compiler_params=pltpu.CompilerParams(
            collective_id=0, has_side_effects=True, vmem_limit_bytes=40 * 1024 * 1024
        ),
        cost_estimate=pl.CostEstimate(flops=flops, bytes_accessed=4 * 1024 * 1024, transcendentals=0),
    )(*[pltpu.with_memory_space_constraint(arg, pltpu.HBM) for arg in args])
    out, vg, kg = pl.pallas_call(
        write_out,
        name="write_out",
        out_shape=(
            jax.ShapeDtypeStruct((256, 128), BF16),
            jax.ShapeDtypeStruct((128, 2, 4, 256), BF16),
            jax.ShapeDtypeStruct((TAPS, 2, TAP_ROWS, 128), F32),
        ),
        in_specs=[vmem] * 3,
        out_specs=(hbm,) * 3,
        scratch_shapes=[dma((2 + 2 * len(RUNS),))],
        compiler_params=pltpu.CompilerParams(vmem_limit_bytes=16 * 1024 * 1024),
    )(out, vg, kg.reshape(2, dims["rows"] // TAP_ROWS, TAP_ROWS, 128))
    return out.reshape(128, 1, 2, 128), vg, kg.reshape(3, 3, 3, 64, 128)


def solution(mesh):
    spec = P(None, "sp", "gz", None)
    return jax.shard_map(
        functools.partial(per_device, layout(mesh)),
        mesh=mesh,
        in_specs=(spec, P(), spec),
        out_specs=(spec, spec, P()),
        check_vma=False,
    )
```

```python
import functools
import math

import jax
import jax.numpy as jnp
from jax import lax
from jax.experimental import pallas as pl
from jax.experimental.pallas import tpu as pltpu
from jax.sharding import PartitionSpec as P

MESH = pl.DeviceIdType.MESH
BF16 = jnp.bfloat16
F32 = jnp.float32
TAP_ROWS = 32
TAPS = 27
POS = {1: 0, 2: 1, 0: 2}


BLOCKS = ((1, 1), (1, 2), (2, 1), (2, 2), (1, 0), (2, 0), (0, 0), (0, 1), (0, 2))
BLOCK_ROWS = 3 * TAP_ROWS
RUNS = ((0, 2), (2, 2), (4, 1), (5, 1), (6, 3))
PARTS = ((0, 4), (4, 9))


def layout(mesh):
    sp, gz = mesh.shape["sp"], mesh.shape["gz"]
    y_lo = 2 if sp >= 32 else 1
    y_hi = 2
    dims = dict(sp=sp, gz=gz, y_lo=y_lo, y_hi=y_hi, z=sp // (2 * y_lo), x=gz // y_hi)
    dims["plane"] = dims["x"] * y_lo * y_hi
    chunks, bases, at = [], [], 0
    for lo, hi in PARTS:
        assert at >= lo * BLOCK_ROWS
        chunks.append(8 * -(-(hi - lo) * BLOCK_ROWS // (8 * dims["plane"])))
        bases.append(at)
        at += chunks[-1] * dims["plane"]
    assert bases[1] == PARTS[1][0] * BLOCK_ROWS
    dims.update(chunks=chunks, bases=bases, rows=at)
    return dims


def body(
    dims, scale, vol_hbm, wgt_hbm, cot_hbm, out, vg, kg,
    vol, wgt, cot, planes, pairs, rows, ups, stack, upst, wl, wt, part, recv_a, recv_b0, recv_b1, recv_c0, recv_c1,
    sends, gets,
    load_s, halo_s, halo_r, a_s, a_r, b_s, b_r, c_s, c_r, e_s, e_r, f_s, f_r,
):
    n_sp, n_gz, n_y_lo, n_z, n_x = (dims[k] for k in ("sp", "gz", "y_lo", "z", "x"))
    n_y = n_y_lo * dims["y_hi"]
    n_plane, chunks, bases = dims["plane"], dims["chunks"], dims["bases"]
    recv_b, recv_c = (recv_b0, recv_b1), (recv_c0, recv_c1)

    loads = [
        pltpu.make_async_copy(src, dst, load_s.at[i])
        for i, (src, dst) in enumerate(((cot_hbm, cot), (vol_hbm, vol), (wgt_hbm, wgt)))
    ]
    for load in loads:
        load.start()

    sp, gz = lax.axis_index("sp"), lax.axis_index("gz")
    core = lax.rem(sp, 2)
    other = 1 - core
    my_z = sp // (2 * n_y_lo)
    my_x = lax.rem(gz, n_x)
    my_y = (gz // n_x) * n_y_lo + lax.rem(sp // 2, n_y_lo)
    me = my_y * n_x + my_x
    partner = (sp + 1 - 2 * core, gz)

    def place(step, sign):
        y = lax.rem(my_y + n_y + sign * (step // n_x), n_y)
        x = lax.rem(my_x + n_x + sign * lax.rem(step, n_x), n_x)
        dev = (my_z * (2 * n_y_lo) + lax.rem(y, n_y_lo) * 2 + core, (y // n_y_lo) * n_x + x)
        return dev, y * n_x + x

    def along_z(step):
        z = lax.rem(my_z + step, n_z)
        return (z * (2 * n_y_lo) + lax.rem(sp, 2 * n_y_lo), gz), z

    def far_plane(i):
        return lax.rem(i + (n_plane // 2 + 1), n_plane - 1) + 1

    def far_z(i):
        return lax.rem(i + max(n_z // 2 - 2, 0), n_z - 1) + 1

    def remote(src, dst, send, recv, dev):
        return pltpu.make_async_remote_copy(
            src_ref=src, dst_ref=dst, send_sem=send, recv_sem=recv, device_id=dev, device_id_type=MESH
        )

    has_prev_sp, has_next_sp = sp > 0, sp < n_sp - 1
    has_prev_gz, has_next_gz = gz > 0, gz < n_gz - 1
    prev_both = jnp.logical_and(has_prev_sp, has_prev_gz)
    next_both = jnp.logical_and(has_next_sp, has_next_gz)

    barrier = pltpu.get_barrier_semaphore()

    def greet(dev):
        pl.semaphore_signal(barrier, inc=1, device_id=dev, device_id_type=MESH)

    near = (
        (has_prev_sp, (sp - 1, gz)),
        (has_next_sp, (sp + 1, gz)),
        (has_prev_gz, (sp, gz - 1)),
        (has_next_gz, (sp, gz + 1)),
        (prev_both, (sp - 1, gz - 1)),
        (next_both, (sp + 1, gz + 1)),
    )
    expected = n_plane - 1 + n_z - 1 + 1
    for cond, dev in near:
        pl.when(cond)(functools.partial(greet, dev))
        expected = expected + cond.astype(jnp.int32)
    greet(partner)

    @pl.loop(0, n_plane - 1, unroll=True)
    def _(i):
        greet(place(far_plane(i), 1)[0])

    @pl.loop(0, n_z - 1, unroll=True)
    def _(i):
        greet(along_z(far_z(i))[0])

    loads[0].wait()
    pairs[...] = cot[...].astype(F32)
    for y in range(2):
        ups[0, y] = pairs[pl.ds(y, 128, stride=2), :].astype(BF16)
    loads[1].wait()
    for j in range(2):
        for z in range(2):
            planes[j, :, 4 * z : 4 * z + 4, :] = vol[:, z, :, 128 * j : 128 * j + 128].astype(F32)
    flat = planes.reshape(2048, 128)
    for z in range(2):
        for y in range(4):
            for j in range(2):
                at = 1024 * j + 4 * z + y
                rows[z, y, :, 128 * j : 128 * j + 128] = flat[pl.ds(at, 128, stride=8), :].astype(BF16)

    halos = (
        (has_prev_gz, has_next_gz, (sp, gz - 1), ups.at[0, 0], ups.at[0, 2]),
        (has_prev_sp, has_next_sp, (sp - 1, gz), ups.at[0, pl.ds(0, 2)], ups.at[1, pl.ds(0, 2)]),
        (prev_both, next_both, (sp - 1, gz - 1), ups.at[0, 0], ups.at[1, 2]),
        (has_next_sp, has_prev_sp, (sp + 1, gz), sends.at[pl.ds(0, 2)], gets.at[pl.ds(0, 2)]),
        (has_next_gz, has_prev_gz, (sp, gz + 1), sends.at[2], gets.at[2]),
        (next_both, prev_both, (sp + 1, gz + 1), sends.at[3], gets.at[3]),
    )
    halo_copies = [
        (to_next, from_prev, remote(src, dst, halo_s.at[i], halo_r.at[i], dev), dst)
        for i, (to_next, from_prev, dev, src, dst) in enumerate(halos)
    ]
    def halo_in(i):
        _, expects, copy, dst = halo_copies[i]
        pl.when(expects)(copy.wait_recv)

        @pl.when(jnp.logical_not(expects))
        def _():
            dst[...] = jnp.zeros(dst.shape, dst.dtype)

    cell = lax.broadcasted_iota(jnp.int32, (256, 384), 0)
    want = lax.broadcasted_iota(jnp.int32, (256, 384), 1)
    want = jnp.where(want < 128, 2 * want, jnp.where(want < 256, 2 * (want - 128) + 1, 2 * (want - 256) - 1))
    split = jnp.where(cell == want, 1.0, 0.0).astype(BF16)
    have = lax.broadcasted_iota(jnp.int32, (256, 256), 0)
    cell = lax.broadcasted_iota(jnp.int32, (256, 256), 1)
    have = jnp.where(have < 128, 2 * have, 2 * (have - 128) + 1)
    join = jnp.where(cell == have, 1.0, 0.0).astype(BF16)

    sets = {0: ((1, 0),), 1: ((0, 1), (2, 0)), 2: ((1, 1),), 3: ((2, 1),)}

    def split_row(p, q):
        cells = jnp.dot(rows[p, q], split, preferred_element_type=F32).astype(BF16)
        for s, half in sets[q]:
            for c in range(3):
                stack[p, s, 128 * c : 128 * c + 128, 128 * half : 128 * half + 128] = cells[:, 128 * c : 128 * c + 128]

    last = lax.broadcasted_iota(jnp.int32, (128, 128), 1) == 127

    def stack_ups(cz, ys):
        for half in range(2):
            here = ups[cz, ys + half]
            ahead = jnp.where(last, 0.0, pltpu.roll(here.astype(F32), 127, 1)).astype(BF16)
            upst[cz, ys, 0:128, 128 * half : 128 * half + 128] = here
            upst[cz, ys, 128:256, 128 * half : 128 * half + 128] = ahead

    first_group = lax.broadcasted_iota(jnp.int32, (64, 128), 1) < 64
    near_of = {0: (2, 1), 1: (1, 0), 2: (2, 0)}
    deep_of = {0: (1, 1), 1: (0, 0), 2: (1, 0)}

    def block_rows(n):
        return pl.ds(n * BLOCK_ROWS, BLOCK_ROWS)

    def core_copy(n):
        return remote(part.at[other, block_rows(n)], recv_a.at[block_rows(n)], a_s.at[n], a_r.at[n], partner)

    def kernel_block(n):
        a, b = BLOCKS[n]
        p, cz = deep_of[a]
        s, ys = near_of[b]
        full_block = lax.dot_general(
            stack[p, s], upst[cz, ys, 0:128, :], (((1,), (1,)), ((), ())), preferred_element_type=F32
        )
        for c in range(3):
            at = 128 * POS[c]
            both = jnp.where(first_group, full_block[at : at + 64], full_block[at + 64 : at + 128])
            to = n * BLOCK_ROWS + c * TAP_ROWS
            part[0, to : to + TAP_ROWS, :] = both[0:TAP_ROWS]
            part[1, to : to + TAP_ROWS, :] = both[TAP_ROWS:]

    def chunk_of(s, k):
        return pl.ds(pl.multiple_of(bases[s] + k * chunks[s], 8), chunks[s])

    def plane_copy(s, d):
        dev, k = place(d, 1)
        return remote(part.at[core, chunk_of(s, k)], recv_b[s].at[d], b_s.at[s], b_r.at[s], dev)

    def plane_all(s):
        got = recv_b[s].at[pl.ds(1, n_plane - 1)]
        return remote(got, got, b_s.at[s], b_r.at[s], partner)

    def z_copy(s, d):
        dev, _ = along_z(d)
        return remote(recv_c[s].at[my_z], recv_c[s].at[my_z], c_s.at[s], c_r.at[s], dev)

    def z_all(s):
        got = recv_c[s].at[pl.ds(1, n_z - 1)]
        return remote(got, got, c_s.at[s], c_r.at[s], partner)

    def back_copy(s, d):
        dev, _ = place(d, 1)
        mine = kg.at[core, chunk_of(s, me)]
        return remote(mine, mine, e_s.at[s], e_r.at[s], dev)

    def back_all(s):
        got = kg.at[core, pl.ds(bases[s], (n_plane - 1) * chunks[s])]
        return remote(got, got, e_s.at[s], e_r.at[s], partner)

    def core_back(s, half):
        where = kg.at[half, pl.ds(bases[s], n_plane * chunks[s])]
        return remote(where, where, f_s.at[s], f_r.at[s], partner)

    def reduce_core(s):
        for n in range(*PARTS[s]):
            core_copy(n).wait_recv()
            part[core, block_rows(n), :] = part[core, block_rows(n), :] + recv_a[block_rows(n), :]

    def start_plane(s):
        @pl.loop(0, n_plane - 1, unroll=True)
        def _(i):
            plane_copy(s, far_plane(i)).start()

    def reduce_plane(s):
        total = part[core, chunk_of(s, me), :]
        plane_all(s).wait_recv()
        for d in range(1, n_plane):
            total = total + recv_b[s][d]
        recv_c[s][my_z] = total

        @pl.loop(0, n_z - 1, unroll=True)
        def _(i):
            z_copy(s, far_z(i)).start()

    def reduce_z(s):
        z_all(s).wait_recv()
        total = recv_c[s][0]
        for z in range(1, n_z):
            total = total + recv_c[s][z]
        kg[core, chunk_of(s, me), :] = total * scale

        @pl.loop(0, n_plane - 1, unroll=True)
        def _(i):
            back_copy(s, far_plane(i)).start()

    real = len(BLOCKS) * BLOCK_ROWS
    if dims["rows"] > real:
        part[:, real:, :] = jnp.zeros((2, dims["rows"] - real, 128), F32)

    stack_ups(0, 0)
    for q in (0, 2):
        for p in (0, 1):
            split_row(p, q)
    kernel_block(0)
    kernel_block(2)
    for q in (1, 3):
        for p in (0, 1):
            split_row(p, q)
    kernel_block(1)
    kernel_block(3)

    pl.semaphore_wait(barrier, expected)


    def start_halos(which):
        for i in which:
            to_next, _, copy, _ = halo_copies[i]
            pl.when(to_next)(copy.start)

    start_halos((0, 1, 2))
    for n in range(*PARTS[0]):
        core_copy(n).start()
    reduce_core(0)
    start_plane(0)

    halo_in(0)
    stack_ups(0, 1)
    for n in (4, 5):
        kernel_block(n)
        core_copy(n).start()
    halo_in(1)
    stack_ups(1, 0)
    for n in (7, 8):
        kernel_block(n)
        core_copy(n).start()
    halo_in(2)
    stack_ups(1, 1)
    kernel_block(6)
    core_copy(6).start()
    reduce_core(1)
    start_plane(1)

    loads[2].wait()
    for tap in range(TAPS):
        a, b, c = tap // 9, (tap // 3) % 3, tap % 3
        w = wgt[64 * tap : 64 * tap + 64, :].astype(F32)
        zero = jnp.zeros_like(w)
        block = jnp.concatenate([jnp.where(first_group, w, zero), jnp.where(first_group, zero, w)], axis=0)
        at = 128 * POS[c]
        wl[3 * a + b, :, at : at + 128] = block.astype(BF16)
        wt[3 * a + b, :, at : at + 128] = block.T.astype(BF16)

    reduce_plane(0)

    for p, deep in ((0, (1,)), (1, (2, 0))):
        for q0, bs in ((0, (1,)), (1, (2, 0))):
            even = odd = None
            for a in deep:
                cz = deep_of[a][1]
                for b in bs:
                    ys = near_of[b][1]
                    e = jnp.dot(wl[3 * a + b, :, 0:128], upst[cz, ys, 0:128, :], preferred_element_type=F32)
                    o = jnp.dot(wl[3 * a + b, :, 128:384], upst[cz, ys], preferred_element_type=F32)
                    even = e if even is None else even + e
                    odd = o if odd is None else odd + o
            for half in range(2):
                lanes = slice(128 * half, 128 * half + 128)
                both = jnp.concatenate([even[:, lanes], odd[:, lanes]], axis=1).astype(BF16)
                cells = jnp.dot(both, join, preferred_element_type=F32)
                for j in range(2):
                    at = 1024 * j + 4 * p + q0 + 2 * half
                    flat[pl.ds(at, 128, stride=8), :] = cells[:, 128 * j : 128 * j + 128]
    for j in range(2):
        for z in range(2):
            vg[:, z, :, 128 * j : 128 * j + 128] = planes[j, :, 4 * z : 4 * z + 4, :].astype(BF16)

    def terms(pairs_of, lanes):
        total = None
        for a, p, b in pairs_of:
            term = jnp.dot(wt[3 * a + b], stack[p, b, :, lanes], preferred_element_type=F32)
            total = term if total is None else total + term
        return total

    for p in (0, 1):
        stack[p, 0, :, 0:128] = jnp.zeros((384, 128), BF16)
    both, ahead = slice(0, 256), slice(128, 256)
    below = terms([(0, 1, b) for b in range(3)], both)
    sends[0] = below[:, 0:128]
    sends[1] = below[:, 128:256]
    sends[2] = jnp.dot(wt[3], stack[0, 2, :, ahead], preferred_element_type=F32) + jnp.dot(
        wt[6], stack[1, 2, :, ahead], preferred_element_type=F32
    )
    sends[3] = jnp.dot(wt[0], stack[1, 2, :, ahead], preferred_element_type=F32)
    mine = terms([(a, a - 1, b) for a in (1, 2) for b in range(3)], both)

    reduce_plane(1)
    reduce_z(0)
    start_halos((3, 4, 5))
    reduce_z(1)

    for i in (3, 4, 5):
        halo_in(i)
    pairs[pl.ds(0, 128, stride=2), :] = mine[:, 0:128] + gets[0] + gets[2] + gets[3]
    pairs[pl.ds(1, 128, stride=2), :] = mine[:, 128:256] + gets[1]
    out[...] = pairs[...].astype(BF16)

    for n in range(len(BLOCKS)):
        core_copy(n).wait_send()
    for to_next, _, copy, _ in halo_copies:
        pl.when(to_next)(copy.wait_send)
    for s in range(2):
        plane_all(s).wait_send()
        z_all(s).wait_send()

    for s in range(2):
        back_all(s).wait_recv()
        core_back(s, core).start()
    for s in range(2):
        back_all(s).wait_send()
        core_back(s, core).wait_send()
        core_back(s, other).wait_recv()


def write_out(out, vg, kg, out_hbm, vg_hbm, kg_hbm, sems):
    copies = [(out, out_hbm), (vg, vg_hbm)]
    for half in range(2):
        for n, count in RUNS:
            a, b = BLOCKS[n]
            copies.append((kg.at[half, pl.ds(3 * n, 3 * count)], kg_hbm.at[pl.ds(9 * a + 3 * b, 3 * count), half]))
    copies = [pltpu.make_async_copy(src, dst, sems.at[i]) for i, (src, dst) in enumerate(copies)]
    for copy in copies:
        copy.start()
    for copy in copies:
        copy.wait()


def per_device(dims, volume, weight, cotangent):
    scale = 1.0 / math.sqrt(dims["sp"] * dims["gz"] * 2 * 128)
    n_plane, n_z, chunks = dims["plane"], dims["z"], dims["chunks"]
    dma = pltpu.SemaphoreType.DMA
    vmem = pl.BlockSpec(memory_space=pltpu.VMEM)
    hbm = pl.BlockSpec(memory_space=pltpu.HBM)
    args = (volume, weight.reshape(TAPS * 64, 128), cotangent.reshape(256, 128))
    flops = 2 * 27 * 64 * 128 * 256 * 3
    out, vg, kg = pl.pallas_call(
        functools.partial(body, dims, scale),
        name="conv_layer",
        out_shape=(
            jax.ShapeDtypeStruct((256, 128), BF16),
            jax.ShapeDtypeStruct((128, 2, 4, 256), BF16),
            jax.ShapeDtypeStruct((2, dims["rows"], 128), F32),
        ),
        in_specs=[hbm] * 3,
        out_specs=(vmem,) * 3,
        scratch_shapes=[
            pltpu.VMEM((128, 2, 4, 256), BF16),
            pltpu.VMEM((TAPS * 64, 128), BF16),
            pltpu.VMEM((256, 128), BF16),
            pltpu.VMEM((2, 128, 8, 128), F32),
            pltpu.VMEM((256, 128), F32),
            pltpu.VMEM((2, 4, 128, 256), BF16),
            pltpu.VMEM((2, 3, 128, 128), BF16),
            pltpu.VMEM((2, 3, 384, 256), BF16),
            pltpu.VMEM((2, 2, 256, 256), BF16),
            pltpu.VMEM((9, 128, 384), BF16),
            pltpu.VMEM((9, 128, 384), BF16),
            pltpu.VMEM((2, dims["rows"], 128), F32),
            pltpu.VMEM((TAPS * TAP_ROWS, 128), F32),
            pltpu.VMEM((n_plane, chunks[0], 128), F32),
            pltpu.VMEM((n_plane, chunks[1], 128), F32),
            pltpu.VMEM((n_z, chunks[0], 128), F32),
            pltpu.VMEM((n_z, chunks[1], 128), F32),
            pltpu.VMEM((4, 128, 128), F32),
            pltpu.VMEM((4, 128, 128), F32),
            dma((3,)),
            dma((6,)), dma((6,)),
            dma((9,)), dma((9,)),
            dma((2,)), dma((2,)),
            dma((2,)), dma((2,)),
            dma((2,)), dma((2,)),
            dma((2,)), dma((2,)),
        ],
        compiler_params=pltpu.CompilerParams(
            collective_id=0, has_side_effects=True, vmem_limit_bytes=40 * 1024 * 1024
        ),
        cost_estimate=pl.CostEstimate(flops=flops, bytes_accessed=4 * 1024 * 1024, transcendentals=0),
    )(*[pltpu.with_memory_space_constraint(arg, pltpu.HBM) for arg in args])
    out, vg, kg = pl.pallas_call(
        write_out,
        name="write_out",
        out_shape=(
            jax.ShapeDtypeStruct((256, 128), BF16),
            jax.ShapeDtypeStruct((128, 2, 4, 256), BF16),
            jax.ShapeDtypeStruct((TAPS, 2, TAP_ROWS, 128), F32),
        ),
        in_specs=[vmem] * 3,
        out_specs=(hbm,) * 3,
        scratch_shapes=[dma((2 + 2 * len(RUNS),))],
        compiler_params=pltpu.CompilerParams(vmem_limit_bytes=16 * 1024 * 1024),
    )(out, vg, kg.reshape(2, dims["rows"] // TAP_ROWS, TAP_ROWS, 128))
    return out.reshape(128, 1, 2, 128), vg, kg.reshape(3, 3, 3, 64, 128)


def solution(mesh):
    spec = P(None, "sp", "gz", None)
    return jax.shard_map(
        functools.partial(per_device, layout(mesh)),
        mesh=mesh,
        in_specs=(spec, P(), spec),
        out_specs=(spec, spec, P()),
        check_vma=False,
    )
```

```python
import functools
import math

import jax
import jax.numpy as jnp
from jax import lax
from jax.experimental import pallas as pl
from jax.experimental.pallas import tpu as pltpu
from jax.sharding import PartitionSpec as P

MESH = pl.DeviceIdType.MESH
BF16 = jnp.bfloat16
F32 = jnp.float32
TAP_ROWS = 32
TAPS = 27
POS = {1: 0, 2: 1, 0: 2}


BLOCKS = ((1, 1), (1, 2), (2, 1), (2, 2), (1, 0), (2, 0), (0, 0), (0, 1), (0, 2))
BLOCK_ROWS = 3 * TAP_ROWS
RUNS = ((0, 2), (2, 2), (4, 1), (5, 1), (6, 3))
PARTS = ((0, 4), (4, 9))


def layout(mesh):
    sp, gz = mesh.shape["sp"], mesh.shape["gz"]
    y_lo = 2 if sp >= 32 else 1
    y_hi = 2
    dims = dict(sp=sp, gz=gz, y_lo=y_lo, y_hi=y_hi, z=sp // (2 * y_lo), x=gz // y_hi)
    dims["plane"] = dims["x"] * y_lo * y_hi
    chunks, bases, at = [], [], 0
    for lo, hi in PARTS:
        assert at >= lo * BLOCK_ROWS
        chunks.append(8 * -(-(hi - lo) * BLOCK_ROWS // (8 * dims["plane"])))
        bases.append(at)
        at += chunks[-1] * dims["plane"]
    assert bases[1] == PARTS[1][0] * BLOCK_ROWS
    dims.update(chunks=chunks, bases=bases, rows=at)
    return dims


def body(
    dims, scale, vol_hbm, wgt_hbm, cot_hbm, out, vg, kg,
    vol, wgt, cot, planes, pairs, rows, ups, stack, upst, wl, wt, part, recv_a, recv_b0, recv_b1, recv_c0, recv_c1,
    sends, gets,
    load_s, halo_s, halo_r, a_s, a_r, b_s, b_r, c_s, c_r, e_s, e_r, f_s, f_r,
):
    n_sp, n_gz, n_y_lo, n_z, n_x = (dims[k] for k in ("sp", "gz", "y_lo", "z", "x"))
    n_y = n_y_lo * dims["y_hi"]
    n_plane, chunks, bases = dims["plane"], dims["chunks"], dims["bases"]
    recv_b, recv_c = (recv_b0, recv_b1), (recv_c0, recv_c1)
    filled = [-(-(hi - lo) * BLOCK_ROWS // chunk) for (lo, hi), chunk in zip(PARTS, chunks)]

    def by_owner(s, owner, rest=None):
        if filled[s] == n_plane:
            owner()
            return
        pl.when(me < filled[s])(owner)
        if rest is not None:
            pl.when(me >= filled[s])(rest)

    loads = [
        pltpu.make_async_copy(src, dst, load_s.at[i])
        for i, (src, dst) in enumerate(((cot_hbm, cot), (vol_hbm, vol), (wgt_hbm, wgt)))
    ]
    for load in loads:
        load.start()

    sp, gz = lax.axis_index("sp"), lax.axis_index("gz")
    core = lax.rem(sp, 2)
    other = 1 - core
    my_z = sp // (2 * n_y_lo)
    my_x = lax.rem(gz, n_x)
    my_y = (gz // n_x) * n_y_lo + lax.rem(sp // 2, n_y_lo)
    me = my_y * n_x + my_x
    partner = (sp + 1 - 2 * core, gz)

    def place(step, sign):
        y = lax.rem(my_y + n_y + sign * (step // n_x), n_y)
        x = lax.rem(my_x + n_x + sign * lax.rem(step, n_x), n_x)
        dev = (my_z * (2 * n_y_lo) + lax.rem(y, n_y_lo) * 2 + core, (y // n_y_lo) * n_x + x)
        return dev, y * n_x + x

    def along_z(step):
        z = lax.rem(my_z + step, n_z)
        return (z * (2 * n_y_lo) + lax.rem(sp, 2 * n_y_lo), gz), z

    def far_plane(i):
        return lax.rem(i + (n_plane // 2 + 1), n_plane - 1) + 1

    def far_z(i):
        return lax.rem(i + max(n_z // 2 - 2, 0), n_z - 1) + 1

    def remote(src, dst, send, recv, dev):
        return pltpu.make_async_remote_copy(
            src_ref=src, dst_ref=dst, send_sem=send, recv_sem=recv, device_id=dev, device_id_type=MESH
        )

    has_prev_sp, has_next_sp = sp > 0, sp < n_sp - 1
    has_prev_gz, has_next_gz = gz > 0, gz < n_gz - 1
    prev_both = jnp.logical_and(has_prev_sp, has_prev_gz)
    next_both = jnp.logical_and(has_next_sp, has_next_gz)

    barrier = pltpu.get_barrier_semaphore()

    def greet(dev):
        pl.semaphore_signal(barrier, inc=1, device_id=dev, device_id_type=MESH)

    near = (
        (has_prev_sp, (sp - 1, gz)),
        (has_next_sp, (sp + 1, gz)),
        (has_prev_gz, (sp, gz - 1)),
        (has_next_gz, (sp, gz + 1)),
        (prev_both, (sp - 1, gz - 1)),
        (next_both, (sp + 1, gz + 1)),
    )
    expected = n_plane - 1 + n_z - 1 + 1
    for cond, dev in near:
        pl.when(cond)(functools.partial(greet, dev))
        expected = expected + cond.astype(jnp.int32)
    greet(partner)

    @pl.loop(0, n_plane - 1, unroll=True)
    def _(i):
        greet(place(far_plane(i), 1)[0])

    @pl.loop(0, n_z - 1, unroll=True)
    def _(i):
        greet(along_z(far_z(i))[0])

    loads[0].wait()
    pairs[...] = cot[...].astype(F32)
    for y in range(2):
        ups[0, y] = pairs[pl.ds(y, 128, stride=2), :].astype(BF16)
    loads[1].wait()
    for j in range(2):
        for z in range(2):
            planes[j, :, 4 * z : 4 * z + 4, :] = vol[:, z, :, 128 * j : 128 * j + 128].astype(F32)
    flat = planes.reshape(2048, 128)
    for z in range(2):
        for y in range(4):
            for j in range(2):
                at = 1024 * j + 4 * z + y
                rows[z, y, :, 128 * j : 128 * j + 128] = flat[pl.ds(at, 128, stride=8), :].astype(BF16)

    halos = (
        (has_prev_gz, has_next_gz, (sp, gz - 1), ups.at[0, 0], ups.at[0, 2]),
        (has_prev_sp, has_next_sp, (sp - 1, gz), ups.at[0, pl.ds(0, 2)], ups.at[1, pl.ds(0, 2)]),
        (prev_both, next_both, (sp - 1, gz - 1), ups.at[0, 0], ups.at[1, 2]),
        (has_next_sp, has_prev_sp, (sp + 1, gz), sends.at[pl.ds(0, 2)], gets.at[pl.ds(0, 2)]),
        (has_next_gz, has_prev_gz, (sp, gz + 1), sends.at[2], gets.at[2]),
        (next_both, prev_both, (sp + 1, gz + 1), sends.at[3], gets.at[3]),
    )
    halo_copies = [
        (to_next, from_prev, remote(src, dst, halo_s.at[i], halo_r.at[i], dev), dst)
        for i, (to_next, from_prev, dev, src, dst) in enumerate(halos)
    ]
    def halo_in(i):
        _, expects, copy, dst = halo_copies[i]
        pl.when(expects)(copy.wait_recv)

        @pl.when(jnp.logical_not(expects))
        def _():
            dst[...] = jnp.zeros(dst.shape, dst.dtype)

    cell = lax.broadcasted_iota(jnp.int32, (256, 384), 0)
    want = lax.broadcasted_iota(jnp.int32, (256, 384), 1)
    want = jnp.where(want < 128, 2 * want, jnp.where(want < 256, 2 * (want - 128) + 1, 2 * (want - 256) - 1))
    split = jnp.where(cell == want, 1.0, 0.0).astype(BF16)
    have = lax.broadcasted_iota(jnp.int32, (256, 256), 0)
    cell = lax.broadcasted_iota(jnp.int32, (256, 256), 1)
    have = jnp.where(have < 128, 2 * have, 2 * (have - 128) + 1)
    join = jnp.where(cell == have, 1.0, 0.0).astype(BF16)

    sets = {0: ((1, 0),), 1: ((0, 1), (2, 0)), 2: ((1, 1),), 3: ((2, 1),)}

    def split_row(p, q):
        cells = jnp.dot(rows[p, q], split, preferred_element_type=F32).astype(BF16)
        for s, half in sets[q]:
            for c in range(3):
                stack[p, s, 128 * c : 128 * c + 128, 128 * half : 128 * half + 128] = cells[:, 128 * c : 128 * c + 128]

    last = lax.broadcasted_iota(jnp.int32, (128, 128), 1) == 127

    def stack_ups(cz, ys):
        for half in range(2):
            here = ups[cz, ys + half]
            ahead = jnp.where(last, 0.0, pltpu.roll(here.astype(F32), 127, 1)).astype(BF16)
            upst[cz, ys, 0:128, 128 * half : 128 * half + 128] = here
            upst[cz, ys, 128:256, 128 * half : 128 * half + 128] = ahead

    first_group = lax.broadcasted_iota(jnp.int32, (64, 128), 1) < 64
    near_of = {0: (2, 1), 1: (1, 0), 2: (2, 0)}
    deep_of = {0: (1, 1), 1: (0, 0), 2: (1, 0)}

    def block_rows(n):
        return pl.ds(n * BLOCK_ROWS, BLOCK_ROWS)

    def core_copy(n):
        return remote(part.at[other, block_rows(n)], recv_a.at[block_rows(n)], a_s.at[n], a_r.at[n], partner)

    def kernel_block(n):
        a, b = BLOCKS[n]
        p, cz = deep_of[a]
        s, ys = near_of[b]
        full_block = lax.dot_general(
            stack[p, s], upst[cz, ys, 0:128, :], (((1,), (1,)), ((), ())), preferred_element_type=F32
        )
        for c in range(3):
            at = 128 * POS[c]
            both = jnp.where(first_group, full_block[at : at + 64], full_block[at + 64 : at + 128])
            to = n * BLOCK_ROWS + c * TAP_ROWS
            part[0, to : to + TAP_ROWS, :] = both[0:TAP_ROWS]
            part[1, to : to + TAP_ROWS, :] = both[TAP_ROWS:]

    def chunk_of(s, k):
        return pl.ds(pl.multiple_of(bases[s] + k * chunks[s], 8), chunks[s])

    def plane_copy(s, d):
        dev, k = place(d, 1)
        return remote(part.at[core, chunk_of(s, k)], recv_b[s].at[d], b_s.at[s], b_r.at[s], dev)

    def plane_all(s, count):
        got = recv_b[s].at[pl.ds(0, count)]
        return remote(got, got, b_s.at[s], b_r.at[s], partner)

    def z_copy(s, d):
        dev, _ = along_z(d)
        return remote(recv_c[s].at[my_z], recv_c[s].at[my_z], c_s.at[s], c_r.at[s], dev)

    def z_all(s):
        got = recv_c[s].at[pl.ds(1, n_z - 1)]
        return remote(got, got, c_s.at[s], c_r.at[s], partner)

    def back_copy(s, d):
        dev, _ = place(d, 1)
        mine = kg.at[core, chunk_of(s, me)]
        return remote(mine, mine, e_s.at[s], e_r.at[s], dev)

    def back_all(s, count):
        got = kg.at[core, pl.ds(bases[s], count * chunks[s])]
        return remote(got, got, e_s.at[s], e_r.at[s], partner)

    def core_back(s, half):
        where = kg.at[half, pl.ds(bases[s], filled[s] * chunks[s])]
        return remote(where, where, f_s.at[s], f_r.at[s], partner)

    def reduce_core(s):
        for n in range(*PARTS[s]):
            core_copy(n).wait_recv()
            part[core, block_rows(n), :] = part[core, block_rows(n), :] + recv_a[block_rows(n), :]

    def start_plane(s):
        @pl.loop(0, n_plane - 1, unroll=True)
        def _(i):
            copy = plane_copy(s, far_plane(i))
            if filled[s] == n_plane:
                copy.start()
            else:
                pl.when(place(far_plane(i), 1)[1] < filled[s])(copy.start)

    def reduce_plane(s):
        def owner():
            total = part[core, chunk_of(s, me), :]
            plane_all(s, n_plane - 1).wait_recv()
            for d in range(1, n_plane):
                total = total + recv_b[s][d]
            recv_c[s][my_z] = total

            @pl.loop(0, n_z - 1, unroll=True)
            def _(i):
                z_copy(s, far_z(i)).start()

        by_owner(s, owner)

    def reduce_z(s):
        def owner():
            z_all(s).wait_recv()
            total = recv_c[s][0]
            for z in range(1, n_z):
                total = total + recv_c[s][z]
            kg[core, chunk_of(s, me), :] = total * scale

            @pl.loop(0, n_plane - 1, unroll=True)
            def _(i):
                back_copy(s, far_plane(i)).start()

        by_owner(s, owner)

    real = len(BLOCKS) * BLOCK_ROWS
    if dims["rows"] > real:
        part[:, real:, :] = jnp.zeros((2, dims["rows"] - real, 128), F32)

    stack_ups(0, 0)
    for q in (0, 2):
        for p in (0, 1):
            split_row(p, q)
    kernel_block(0)
    kernel_block(2)
    for q in (1, 3):
        for p in (0, 1):
            split_row(p, q)
    kernel_block(1)
    kernel_block(3)

    pl.semaphore_wait(barrier, expected)


    def start_halos(which):
        for i in which:
            to_next, _, copy, _ = halo_copies[i]
            pl.when(to_next)(copy.start)

    start_halos((0, 1, 2))
    for n in range(*PARTS[0]):
        core_copy(n).start()
    reduce_core(0)
    start_plane(0)

    halo_in(0)
    stack_ups(0, 1)
    for n in (4, 5):
        kernel_block(n)
        core_copy(n).start()
    halo_in(1)
    stack_ups(1, 0)
    for n in (7, 8):
        kernel_block(n)
        core_copy(n).start()
    halo_in(2)
    stack_ups(1, 1)
    kernel_block(6)
    core_copy(6).start()
    reduce_core(1)
    start_plane(1)

    loads[2].wait()
    for tap in range(TAPS):
        a, b, c = tap // 9, (tap // 3) % 3, tap % 3
        w = wgt[64 * tap : 64 * tap + 64, :].astype(F32)
        zero = jnp.zeros_like(w)
        block = jnp.concatenate([jnp.where(first_group, w, zero), jnp.where(first_group, zero, w)], axis=0)
        at = 128 * POS[c]
        wl[3 * a + b, :, at : at + 128] = block.astype(BF16)
        wt[3 * a + b, :, at : at + 128] = block.T.astype(BF16)

    reduce_plane(0)

    for p, deep in ((0, (1,)), (1, (2, 0))):
        for q0, bs in ((0, (1,)), (1, (2, 0))):
            even = odd = None
            for a in deep:
                cz = deep_of[a][1]
                for b in bs:
                    ys = near_of[b][1]
                    e = jnp.dot(wl[3 * a + b, :, 0:128], upst[cz, ys, 0:128, :], preferred_element_type=F32)
                    o = jnp.dot(wl[3 * a + b, :, 128:384], upst[cz, ys], preferred_element_type=F32)
                    even = e if even is None else even + e
                    odd = o if odd is None else odd + o
            for half in range(2):
                lanes = slice(128 * half, 128 * half + 128)
                both = jnp.concatenate([even[:, lanes], odd[:, lanes]], axis=1).astype(BF16)
                cells = jnp.dot(both, join, preferred_element_type=F32)
                for j in range(2):
                    at = 1024 * j + 4 * p + q0 + 2 * half
                    flat[pl.ds(at, 128, stride=8), :] = cells[:, 128 * j : 128 * j + 128]
    for j in range(2):
        for z in range(2):
            vg[:, z, :, 128 * j : 128 * j + 128] = planes[j, :, 4 * z : 4 * z + 4, :].astype(BF16)

    def terms(pairs_of, lanes):
        total = None
        for a, p, b in pairs_of:
            term = jnp.dot(wt[3 * a + b], stack[p, b, :, lanes], preferred_element_type=F32)
            total = term if total is None else total + term
        return total

    for p in (0, 1):
        stack[p, 0, :, 0:128] = jnp.zeros((384, 128), BF16)
    both, ahead = slice(0, 256), slice(128, 256)
    below = terms([(0, 1, b) for b in range(3)], both)
    sends[0] = below[:, 0:128]
    sends[1] = below[:, 128:256]
    sends[2] = jnp.dot(wt[3], stack[0, 2, :, ahead], preferred_element_type=F32) + jnp.dot(
        wt[6], stack[1, 2, :, ahead], preferred_element_type=F32
    )
    sends[3] = jnp.dot(wt[0], stack[1, 2, :, ahead], preferred_element_type=F32)
    mine = terms([(a, a - 1, b) for a in (1, 2) for b in range(3)], both)

    reduce_plane(1)
    reduce_z(0)
    start_halos((3, 4, 5))
    reduce_z(1)

    for i in (3, 4, 5):
        halo_in(i)
    pairs[pl.ds(0, 128, stride=2), :] = mine[:, 0:128] + gets[0] + gets[2] + gets[3]
    pairs[pl.ds(1, 128, stride=2), :] = mine[:, 128:256] + gets[1]
    out[...] = pairs[...].astype(BF16)

    for n in range(len(BLOCKS)):
        core_copy(n).wait_send()
    for to_next, _, copy, _ in halo_copies:
        pl.when(to_next)(copy.wait_send)
    for s in range(2):
        by_owner(
            s,
            lambda: (plane_all(s, filled[s] - 1).wait_send(), z_all(s).wait_send(), None)[-1],
            lambda: plane_all(s, filled[s]).wait_send(),
        )

    for s in range(2):
        by_owner(s, lambda: back_all(s, filled[s] - 1).wait_recv(), lambda: back_all(s, filled[s]).wait_recv())
        core_back(s, core).start()
    for s in range(2):
        by_owner(s, lambda: back_all(s, n_plane - 1).wait_send())
        core_back(s, core).wait_send()
        core_back(s, other).wait_recv()


def write_out(out, vg, kg, out_hbm, vg_hbm, kg_hbm, sems):
    copies = []
    for half in range(2):
        for n, count in RUNS:
            a, b = BLOCKS[n]
            copies.append((kg.at[half, pl.ds(3 * n, 3 * count)], kg_hbm.at[pl.ds(9 * a + 3 * b, 3 * count), half]))
    copies += [(vg, vg_hbm), (out, out_hbm)]
    copies = [pltpu.make_async_copy(src, dst, sems.at[i]) for i, (src, dst) in enumerate(copies)]
    for copy in copies:
        copy.start()
    for copy in copies:
        copy.wait()


def per_device(dims, volume, weight, cotangent):
    scale = 1.0 / math.sqrt(dims["sp"] * dims["gz"] * 2 * 128)
    n_plane, n_z, chunks = dims["plane"], dims["z"], dims["chunks"]
    dma = pltpu.SemaphoreType.DMA
    vmem = pl.BlockSpec(memory_space=pltpu.VMEM)
    hbm = pl.BlockSpec(memory_space=pltpu.HBM)
    args = (volume, weight.reshape(TAPS * 64, 128), cotangent.reshape(256, 128))
    flops = 2 * 27 * 64 * 128 * 256 * 3
    out, vg, kg = pl.pallas_call(
        functools.partial(body, dims, scale),
        name="conv_layer",
        out_shape=(
            jax.ShapeDtypeStruct((256, 128), BF16),
            jax.ShapeDtypeStruct((128, 2, 4, 256), BF16),
            jax.ShapeDtypeStruct((2, dims["rows"], 128), F32),
        ),
        in_specs=[hbm] * 3,
        out_specs=(vmem,) * 3,
        scratch_shapes=[
            pltpu.VMEM((128, 2, 4, 256), BF16),
            pltpu.VMEM((TAPS * 64, 128), BF16),
            pltpu.VMEM((256, 128), BF16),
            pltpu.VMEM((2, 128, 8, 128), F32),
            pltpu.VMEM((256, 128), F32),
            pltpu.VMEM((2, 4, 128, 256), BF16),
            pltpu.VMEM((2, 3, 128, 128), BF16),
            pltpu.VMEM((2, 3, 384, 256), BF16),
            pltpu.VMEM((2, 2, 256, 256), BF16),
            pltpu.VMEM((9, 128, 384), BF16),
            pltpu.VMEM((9, 128, 384), BF16),
            pltpu.VMEM((2, dims["rows"], 128), F32),
            pltpu.VMEM((TAPS * TAP_ROWS, 128), F32),
            pltpu.VMEM((n_plane, chunks[0], 128), F32),
            pltpu.VMEM((n_plane, chunks[1], 128), F32),
            pltpu.VMEM((n_z, chunks[0], 128), F32),
            pltpu.VMEM((n_z, chunks[1], 128), F32),
            pltpu.VMEM((4, 128, 128), F32),
            pltpu.VMEM((4, 128, 128), F32),
            dma((3,)),
            dma((6,)), dma((6,)),
            dma((9,)), dma((9,)),
            dma((2,)), dma((2,)),
            dma((2,)), dma((2,)),
            dma((2,)), dma((2,)),
            dma((2,)), dma((2,)),
        ],
        compiler_params=pltpu.CompilerParams(
            collective_id=0, has_side_effects=True, vmem_limit_bytes=40 * 1024 * 1024
        ),
        cost_estimate=pl.CostEstimate(flops=flops, bytes_accessed=4 * 1024 * 1024, transcendentals=0),
    )(*[pltpu.with_memory_space_constraint(arg, pltpu.HBM) for arg in args])
    out, vg, kg = pl.pallas_call(
        write_out,
        name="write_out",
        out_shape=(
            jax.ShapeDtypeStruct((256, 128), BF16),
            jax.ShapeDtypeStruct((128, 2, 4, 256), BF16),
            jax.ShapeDtypeStruct((TAPS, 2, TAP_ROWS, 128), F32),
        ),
        in_specs=[vmem] * 3,
        out_specs=(hbm,) * 3,
        scratch_shapes=[dma((2 + 2 * len(RUNS),))],
        compiler_params=pltpu.CompilerParams(vmem_limit_bytes=16 * 1024 * 1024),
    )(out, vg, kg.reshape(2, dims["rows"] // TAP_ROWS, TAP_ROWS, 128))
    return out.reshape(128, 1, 2, 128), vg, kg.reshape(3, 3, 3, 64, 128)


def solution(mesh):
    spec = P(None, "sp", "gz", None)
    return jax.shard_map(
        functools.partial(per_device, layout(mesh)),
        mesh=mesh,
        in_specs=(spec, P(), spec),
        out_specs=(spec, spec, P()),
        check_vma=False,
    )
```

```python
import functools
import math

import jax
import jax.numpy as jnp
from jax import lax
from jax.experimental import pallas as pl
from jax.experimental.pallas import tpu as pltpu
from jax.sharding import PartitionSpec as P

MESH = pl.DeviceIdType.MESH
BF16 = jnp.bfloat16
F32 = jnp.float32
TAP_ROWS = 32
TAPS = 27
POS = {1: 0, 2: 1, 0: 2}


BLOCKS = ((1, 1), (1, 2), (2, 1), (2, 2), (1, 0), (2, 0), (0, 0), (0, 1), (0, 2))
BLOCK_ROWS = 3 * TAP_ROWS
RUNS = ((0, 2), (2, 2), (4, 1), (5, 1), (6, 3))
PARTS = ((0, 4), (4, 9))


def layout(mesh):
    sp, gz = mesh.shape["sp"], mesh.shape["gz"]
    y_lo = 2 if sp >= 32 else 1
    y_hi = 2
    dims = dict(sp=sp, gz=gz, y_lo=y_lo, y_hi=y_hi, z=sp // (2 * y_lo), x=gz // y_hi)
    dims["plane"] = dims["x"] * y_lo * y_hi
    chunks, bases, at = [], [], 0
    for lo, hi in PARTS:
        assert at >= lo * BLOCK_ROWS
        chunks.append(8 * -(-(hi - lo) * BLOCK_ROWS // (8 * dims["plane"])))
        bases.append(at)
        at += chunks[-1] * dims["plane"]
    assert bases[1] == PARTS[1][0] * BLOCK_ROWS
    dims.update(chunks=chunks, bases=bases, rows=at)
    return dims


def body(
    dims, scale, vol_hbm, wgt_hbm, cot_hbm, out, vg, kg,
    vol, wgt, cot, planes, pairs, rows, ups, stack, upst, wl, wt, part, recv_a, recv_b0, recv_b1, recv_c0, recv_c1,
    sends, gets,
    load_s, halo_s, halo_r, a_s, a_r, b_s, b_r, c_s, c_r, e_s, e_r, f_s, f_r,
):
    n_sp, n_gz, n_y_lo, n_z, n_x = (dims[k] for k in ("sp", "gz", "y_lo", "z", "x"))
    n_y = n_y_lo * dims["y_hi"]
    n_plane, chunks, bases = dims["plane"], dims["chunks"], dims["bases"]
    recv_b, recv_c = (recv_b0, recv_b1), (recv_c0, recv_c1)

    loads = [
        pltpu.make_async_copy(src, dst, load_s.at[i])
        for i, (src, dst) in enumerate(((cot_hbm, cot), (vol_hbm, vol), (wgt_hbm, wgt)))
    ]
    for load in loads:
        load.start()

    sp, gz = lax.axis_index("sp"), lax.axis_index("gz")
    core = lax.rem(sp, 2)
    other = 1 - core
    my_z = sp // (2 * n_y_lo)
    my_x = lax.rem(gz, n_x)
    my_y = (gz // n_x) * n_y_lo + lax.rem(sp // 2, n_y_lo)
    me = my_y * n_x + my_x
    partner = (sp + 1 - 2 * core, gz)

    def place(step, sign):
        y = lax.rem(my_y + n_y + sign * (step // n_x), n_y)
        x = lax.rem(my_x + n_x + sign * lax.rem(step, n_x), n_x)
        dev = (my_z * (2 * n_y_lo) + lax.rem(y, n_y_lo) * 2 + core, (y // n_y_lo) * n_x + x)
        return dev, y * n_x + x

    def along_z(step):
        z = lax.rem(my_z + step, n_z)
        return (z * (2 * n_y_lo) + lax.rem(sp, 2 * n_y_lo), gz), z

    def way(step):
        x, y = step % n_x, step // n_x
        return min(x, n_x - x) + min(y, n_y - y)

    far_plane = sorted(range(1, n_plane), key=way, reverse=True)
    far_z = sorted(range(1, n_z), key=lambda d: min(d, n_z - d), reverse=True)

    def remote(src, dst, send, recv, dev):
        return pltpu.make_async_remote_copy(
            src_ref=src, dst_ref=dst, send_sem=send, recv_sem=recv, device_id=dev, device_id_type=MESH
        )

    has_prev_sp, has_next_sp = sp > 0, sp < n_sp - 1
    has_prev_gz, has_next_gz = gz > 0, gz < n_gz - 1
    prev_both = jnp.logical_and(has_prev_sp, has_prev_gz)
    next_both = jnp.logical_and(has_next_sp, has_next_gz)

    barrier = pltpu.get_barrier_semaphore()

    def greet(dev):
        pl.semaphore_signal(barrier, inc=1, device_id=dev, device_id_type=MESH)

    near = (
        (has_prev_sp, (sp - 1, gz)),
        (has_next_sp, (sp + 1, gz)),
        (has_prev_gz, (sp, gz - 1)),
        (has_next_gz, (sp, gz + 1)),
        (prev_both, (sp - 1, gz - 1)),
        (next_both, (sp + 1, gz + 1)),
    )
    expected = n_plane - 1 + n_z - 1 + 1
    for cond, dev in near:
        pl.when(cond)(functools.partial(greet, dev))
        expected = expected + cond.astype(jnp.int32)
    greet(partner)

    for d in far_plane:
        greet(place(d, 1)[0])

    for d in far_z:
        greet(along_z(d)[0])

    loads[0].wait()
    pairs[...] = cot[...].astype(F32)
    for y in range(2):
        ups[0, y] = pairs[pl.ds(y, 128, stride=2), :].astype(BF16)
    loads[1].wait()
    for j in range(2):
        for z in range(2):
            planes[j, :, 4 * z : 4 * z + 4, :] = vol[:, z, :, 128 * j : 128 * j + 128].astype(F32)
    flat = planes.reshape(2048, 128)
    for z in range(2):
        for y in range(4):
            for j in range(2):
                at = 1024 * j + 4 * z + y
                rows[z, y, :, 128 * j : 128 * j + 128] = flat[pl.ds(at, 128, stride=8), :].astype(BF16)

    halos = (
        (has_prev_gz, has_next_gz, (sp, gz - 1), ups.at[0, 0], ups.at[0, 2]),
        (has_prev_sp, has_next_sp, (sp - 1, gz), ups.at[0, pl.ds(0, 2)], ups.at[1, pl.ds(0, 2)]),
        (prev_both, next_both, (sp - 1, gz - 1), ups.at[0, 0], ups.at[1, 2]),
        (has_next_sp, has_prev_sp, (sp + 1, gz), sends.at[pl.ds(0, 2)], gets.at[pl.ds(0, 2)]),
        (has_next_gz, has_prev_gz, (sp, gz + 1), sends.at[2], gets.at[2]),
        (next_both, prev_both, (sp + 1, gz + 1), sends.at[3], gets.at[3]),
    )
    halo_copies = [
        (to_next, from_prev, remote(src, dst, halo_s.at[i], halo_r.at[i], dev), dst)
        for i, (to_next, from_prev, dev, src, dst) in enumerate(halos)
    ]
    def halo_in(i):
        _, expects, copy, dst = halo_copies[i]
        pl.when(expects)(copy.wait_recv)

        @pl.when(jnp.logical_not(expects))
        def _():
            dst[...] = jnp.zeros(dst.shape, dst.dtype)

    cell = lax.broadcasted_iota(jnp.int32, (256, 384), 0)
    want = lax.broadcasted_iota(jnp.int32, (256, 384), 1)
    want = jnp.where(want < 128, 2 * want, jnp.where(want < 256, 2 * (want - 128) + 1, 2 * (want - 256) - 1))
    split = jnp.where(cell == want, 1.0, 0.0).astype(BF16)
    have = lax.broadcasted_iota(jnp.int32, (256, 256), 0)
    cell = lax.broadcasted_iota(jnp.int32, (256, 256), 1)
    have = jnp.where(have < 128, 2 * have, 2 * (have - 128) + 1)
    join = jnp.where(cell == have, 1.0, 0.0).astype(BF16)

    sets = {0: ((1, 0),), 1: ((0, 1), (2, 0)), 2: ((1, 1),), 3: ((2, 1),)}

    def split_row(p, q):
        cells = jnp.dot(rows[p, q], split, preferred_element_type=F32).astype(BF16)
        for s, half in sets[q]:
            for c in range(3):
                stack[p, s, 128 * c : 128 * c + 128, 128 * half : 128 * half + 128] = cells[:, 128 * c : 128 * c + 128]

    last = lax.broadcasted_iota(jnp.int32, (128, 128), 1) == 127

    def stack_ups(cz, ys):
        for half in range(2):
            here = ups[cz, ys + half]
            ahead = jnp.where(last, 0.0, pltpu.roll(here.astype(F32), 127, 1)).astype(BF16)
            upst[cz, ys, 0:128, 128 * half : 128 * half + 128] = here
            upst[cz, ys, 128:256, 128 * half : 128 * half + 128] = ahead

    first_group = lax.broadcasted_iota(jnp.int32, (64, 128), 1) < 64
    near_of = {0: (2, 1), 1: (1, 0), 2: (2, 0)}
    deep_of = {0: (1, 1), 1: (0, 0), 2: (1, 0)}

    def block_rows(n):
        return pl.ds(n * BLOCK_ROWS, BLOCK_ROWS)

    def core_copy(n):
        return remote(part.at[other, block_rows(n)], recv_a.at[block_rows(n)], a_s.at[n], a_r.at[n], partner)

    def kernel_block(n):
        a, b = BLOCKS[n]
        p, cz = deep_of[a]
        s, ys = near_of[b]
        full_block = lax.dot_general(
            stack[p, s], upst[cz, ys, 0:128, :], (((1,), (1,)), ((), ())), preferred_element_type=F32
        )
        for c in range(3):
            at = 128 * POS[c]
            both = jnp.where(first_group, full_block[at : at + 64], full_block[at + 64 : at + 128])
            to = n * BLOCK_ROWS + c * TAP_ROWS
            part[0, to : to + TAP_ROWS, :] = both[0:TAP_ROWS]
            part[1, to : to + TAP_ROWS, :] = both[TAP_ROWS:]

    def chunk_of(s, k):
        return pl.ds(pl.multiple_of(bases[s] + k * chunks[s], 8), chunks[s])

    def plane_copy(s, d):
        dev, k = place(d, 1)
        return remote(part.at[core, chunk_of(s, k)], recv_b[s].at[d], b_s.at[s], b_r.at[s], dev)

    def plane_all(s):
        got = recv_b[s].at[pl.ds(1, n_plane - 1)]
        return remote(got, got, b_s.at[s], b_r.at[s], partner)

    def z_copy(s, d):
        dev, _ = along_z(d)
        return remote(recv_c[s].at[my_z], recv_c[s].at[my_z], c_s.at[s], c_r.at[s], dev)

    def z_all(s):
        got = recv_c[s].at[pl.ds(1, n_z - 1)]
        return remote(got, got, c_s.at[s], c_r.at[s], partner)

    def back_copy(s, d):
        dev, _ = place(d, 1)
        mine = kg.at[core, chunk_of(s, me)]
        return remote(mine, mine, e_s.at[s], e_r.at[s], dev)

    def back_all(s):
        got = kg.at[core, pl.ds(bases[s], (n_plane - 1) * chunks[s])]
        return remote(got, got, e_s.at[s], e_r.at[s], partner)

    def core_back(s, half):
        where = kg.at[half, pl.ds(bases[s], n_plane * chunks[s])]
        return remote(where, where, f_s.at[s], f_r.at[s], partner)

    def reduce_core(s):
        for n in range(*PARTS[s]):
            core_copy(n).wait_recv()
            part[core, block_rows(n), :] = part[core, block_rows(n), :] + recv_a[block_rows(n), :]

    def start_plane(s):
        for d in far_plane:
            plane_copy(s, d).start()

    def reduce_plane(s):
        total = part[core, chunk_of(s, me), :]
        plane_all(s).wait_recv()
        for d in range(1, n_plane):
            total = total + recv_b[s][d]
        recv_c[s][my_z] = total

        for d in far_z:
            z_copy(s, d).start()

    def reduce_z(s):
        z_all(s).wait_recv()
        total = recv_c[s][0]
        for z in range(1, n_z):
            total = total + recv_c[s][z]
        kg[core, chunk_of(s, me), :] = total * scale

        for d in far_plane:
            back_copy(s, d).start()

    real = len(BLOCKS) * BLOCK_ROWS
    if dims["rows"] > real:
        part[:, real:, :] = jnp.zeros((2, dims["rows"] - real, 128), F32)

    stack_ups(0, 0)
    for q in (0, 2):
        for p in (0, 1):
            split_row(p, q)
    kernel_block(0)
    kernel_block(2)
    for q in (1, 3):
        for p in (0, 1):
            split_row(p, q)
    kernel_block(1)
    kernel_block(3)

    pl.semaphore_wait(barrier, expected)


    def start_halos(which):
        for i in which:
            to_next, _, copy, _ = halo_copies[i]
            pl.when(to_next)(copy.start)

    start_halos((0, 1, 2))
    for n in range(*PARTS[0]):
        core_copy(n).start()
    reduce_core(0)
    start_plane(0)

    halo_in(0)
    stack_ups(0, 1)
    for n in (4, 5):
        kernel_block(n)
        core_copy(n).start()
    halo_in(1)
    stack_ups(1, 0)
    for n in (7, 8):
        kernel_block(n)
        core_copy(n).start()
    halo_in(2)
    stack_ups(1, 1)
    kernel_block(6)
    core_copy(6).start()
    reduce_core(1)
    start_plane(1)

    loads[2].wait()
    for tap in range(TAPS):
        a, b, c = tap // 9, (tap // 3) % 3, tap % 3
        w = wgt[64 * tap : 64 * tap + 64, :].astype(F32)
        zero = jnp.zeros_like(w)
        block = jnp.concatenate([jnp.where(first_group, w, zero), jnp.where(first_group, zero, w)], axis=0)
        at = 128 * POS[c]
        wl[3 * a + b, :, at : at + 128] = block.astype(BF16)
        wt[3 * a + b, :, at : at + 128] = block.T.astype(BF16)

    reduce_plane(0)

    for p, deep in ((0, (1,)), (1, (2, 0))):
        for q0, bs in ((0, (1,)), (1, (2, 0))):
            even = odd = None
            for a in deep:
                cz = deep_of[a][1]
                for b in bs:
                    ys = near_of[b][1]
                    e = jnp.dot(wl[3 * a + b, :, 0:128], upst[cz, ys, 0:128, :], preferred_element_type=F32)
                    o = jnp.dot(wl[3 * a + b, :, 128:384], upst[cz, ys], preferred_element_type=F32)
                    even = e if even is None else even + e
                    odd = o if odd is None else odd + o
            for half in range(2):
                lanes = slice(128 * half, 128 * half + 128)
                both = jnp.concatenate([even[:, lanes], odd[:, lanes]], axis=1).astype(BF16)
                cells = jnp.dot(both, join, preferred_element_type=F32)
                for j in range(2):
                    at = 1024 * j + 4 * p + q0 + 2 * half
                    flat[pl.ds(at, 128, stride=8), :] = cells[:, 128 * j : 128 * j + 128]
    for j in range(2):
        for z in range(2):
            vg[:, z, :, 128 * j : 128 * j + 128] = planes[j, :, 4 * z : 4 * z + 4, :].astype(BF16)

    def terms(pairs_of, lanes):
        total = None
        for a, p, b in pairs_of:
            term = jnp.dot(wt[3 * a + b], stack[p, b, :, lanes], preferred_element_type=F32)
            total = term if total is None else total + term
        return total

    for p in (0, 1):
        stack[p, 0, :, 0:128] = jnp.zeros((384, 128), BF16)
    both, ahead = slice(0, 256), slice(128, 256)
    below = terms([(0, 1, b) for b in range(3)], both)
    sends[0] = below[:, 0:128]
    sends[1] = below[:, 128:256]
    sends[2] = jnp.dot(wt[3], stack[0, 2, :, ahead], preferred_element_type=F32) + jnp.dot(
        wt[6], stack[1, 2, :, ahead], preferred_element_type=F32
    )
    sends[3] = jnp.dot(wt[0], stack[1, 2, :, ahead], preferred_element_type=F32)
    mine = terms([(a, a - 1, b) for a in (1, 2) for b in range(3)], both)

    reduce_plane(1)
    reduce_z(0)
    start_halos((3, 4, 5))
    reduce_z(1)

    for i in (3, 4, 5):
        halo_in(i)
    pairs[pl.ds(0, 128, stride=2), :] = mine[:, 0:128] + gets[0] + gets[2] + gets[3]
    pairs[pl.ds(1, 128, stride=2), :] = mine[:, 128:256] + gets[1]
    out[...] = pairs[...].astype(BF16)

    for n in range(len(BLOCKS)):
        core_copy(n).wait_send()
    for to_next, _, copy, _ in halo_copies:
        pl.when(to_next)(copy.wait_send)
    for s in range(2):
        plane_all(s).wait_send()
        z_all(s).wait_send()

    for s in range(2):
        back_all(s).wait_recv()
        core_back(s, core).start()
    for s in range(2):
        back_all(s).wait_send()
        core_back(s, core).wait_send()
        core_back(s, other).wait_recv()


def write_out(out, vg, kg, out_hbm, vg_hbm, kg_hbm, sems):
    copies = [(out, out_hbm), (vg, vg_hbm)]
    for half in range(2):
        for n, count in RUNS:
            a, b = BLOCKS[n]
            copies.append((kg.at[half, pl.ds(3 * n, 3 * count)], kg_hbm.at[pl.ds(9 * a + 3 * b, 3 * count), half]))
    copies = [pltpu.make_async_copy(src, dst, sems.at[i]) for i, (src, dst) in enumerate(copies)]
    for copy in copies:
        copy.start()
    for copy in copies:
        copy.wait()


def per_device(dims, volume, weight, cotangent):
    scale = 1.0 / math.sqrt(dims["sp"] * dims["gz"] * 2 * 128)
    n_plane, n_z, chunks = dims["plane"], dims["z"], dims["chunks"]
    dma = pltpu.SemaphoreType.DMA
    vmem = pl.BlockSpec(memory_space=pltpu.VMEM)
    hbm = pl.BlockSpec(memory_space=pltpu.HBM)
    args = (volume, weight.reshape(TAPS * 64, 128), cotangent.reshape(256, 128))
    flops = 2 * 27 * 64 * 128 * 256 * 3
    out, vg, kg = pl.pallas_call(
        functools.partial(body, dims, scale),
        name="conv_layer",
        out_shape=(
            jax.ShapeDtypeStruct((256, 128), BF16),
            jax.ShapeDtypeStruct((128, 2, 4, 256), BF16),
            jax.ShapeDtypeStruct((2, dims["rows"], 128), F32),
        ),
        in_specs=[hbm] * 3,
        out_specs=(vmem,) * 3,
        scratch_shapes=[
            pltpu.VMEM((128, 2, 4, 256), BF16),
            pltpu.VMEM((TAPS * 64, 128), BF16),
            pltpu.VMEM((256, 128), BF16),
            pltpu.VMEM((2, 128, 8, 128), F32),
            pltpu.VMEM((256, 128), F32),
            pltpu.VMEM((2, 4, 128, 256), BF16),
            pltpu.VMEM((2, 3, 128, 128), BF16),
            pltpu.VMEM((2, 3, 384, 256), BF16),
            pltpu.VMEM((2, 2, 256, 256), BF16),
            pltpu.VMEM((9, 128, 384), BF16),
            pltpu.VMEM((9, 128, 384), BF16),
            pltpu.VMEM((2, dims["rows"], 128), F32),
            pltpu.VMEM((TAPS * TAP_ROWS, 128), F32),
            pltpu.VMEM((n_plane, chunks[0], 128), F32),
            pltpu.VMEM((n_plane, chunks[1], 128), F32),
            pltpu.VMEM((n_z, chunks[0], 128), F32),
            pltpu.VMEM((n_z, chunks[1], 128), F32),
            pltpu.VMEM((4, 128, 128), F32),
            pltpu.VMEM((4, 128, 128), F32),
            dma((3,)),
            dma((6,)), dma((6,)),
            dma((9,)), dma((9,)),
            dma((2,)), dma((2,)),
            dma((2,)), dma((2,)),
            dma((2,)), dma((2,)),
            dma((2,)), dma((2,)),
        ],
        compiler_params=pltpu.CompilerParams(
            collective_id=0, has_side_effects=True, vmem_limit_bytes=40 * 1024 * 1024
        ),
        cost_estimate=pl.CostEstimate(flops=flops, bytes_accessed=4 * 1024 * 1024, transcendentals=0),
    )(*[pltpu.with_memory_space_constraint(arg, pltpu.HBM) for arg in args])
    out, vg, kg = pl.pallas_call(
        write_out,
        name="write_out",
        out_shape=(
            jax.ShapeDtypeStruct((256, 128), BF16),
            jax.ShapeDtypeStruct((128, 2, 4, 256), BF16),
            jax.ShapeDtypeStruct((TAPS, 2, TAP_ROWS, 128), F32),
        ),
        in_specs=[vmem] * 3,
        out_specs=(hbm,) * 3,
        scratch_shapes=[dma((2 + 2 * len(RUNS),))],
        compiler_params=pltpu.CompilerParams(vmem_limit_bytes=16 * 1024 * 1024),
    )(out, vg, kg.reshape(2, dims["rows"] // TAP_ROWS, TAP_ROWS, 128))
    return out.reshape(128, 1, 2, 128), vg, kg.reshape(3, 3, 3, 64, 128)


def solution(mesh):
    spec = P(None, "sp", "gz", None)
    return jax.shard_map(
        functools.partial(per_device, layout(mesh)),
        mesh=mesh,
        in_specs=(spec, P(), spec),
        out_specs=(spec, spec, P()),
        check_vma=False,
    )
```
